32 devices in a mesh: ex: 2 (over core), ey: 16 (over z, y, x).
Axes of the slice: x: 2, y: 2, z: 4, core: 2. Of those that a mesh axis runs over, the one named last changes fastest.
Arguments:
- tokens: bfloat16 [32, 256, 1024], P(('ex', 'ey')), may hold values from -16 to 16
- slot_param: bfloat16 [1024, 32], replicated, may hold values from -0.75 to 0.75
- weight_in: bfloat16 [32, 1024, 4096], P('ey', None, 'ex'), may hold values from -0.1875 to 0.1875
- weight_out: bfloat16 [32, 4096, 1024], P('ey', 'ex'), may hold values from -0.09375 to 0.09375
- grad_out: bfloat16 [32, 256, 1024], P(('ex', 'ey')), may hold values from -6 to 6
Outputs:
- grad_tokens: bfloat16 [32, 256, 1024], P(('ex', 'ey'))
- grad_param: float32 [1024, 32], replicated
- grad_win: bfloat16 [32, 1024, 4096], P('ey', None, 'ex')
- grad_wout: bfloat16 [32, 4096, 1024], P('ey', 'ex')
The draws below stay inside these ranges and needn't reach their ends.
All inputs are finite; a program needn't handle non-finite values.
Results may differ from the reference program's by a relative error of at most 0.017.
Values may be sent and summed in bfloat16 or wider, within the bound.
No kernel may reach another device: no remote copies, remote signals or barrier semaphores. Data moves between devices by JAX's collectives and lax.ppermute only.
A program may use at most 64 MiB of HBM per device.

```python
import jax
import jax.numpy as jnp
from jax import lax

D = 1024
FF = 4096
PATCHES = 256
EXPERTS = 32
IMAGES = 32


def slot_table(key):
    raw = 0.125 * jax.random.normal(jax.random.fold_in(key, 11), (D, EXPERTS), jnp.float32)
    return jnp.clip(raw, -0.75, 0.75)


def draw_slot_param(key, part):
    return slot_table(key).astype(jnp.bfloat16)


def draw_tokens(key, part):
    shape = (IMAGES, PATCHES, D)
    base = jax.random.normal(jax.random.fold_in(key, 3), shape, jnp.float32)
    return jnp.clip(base, -6.0, 6.0).astype(jnp.bfloat16)


def block_scale(stream_key, dims, shards, low, high):
    gain, own = 1.0, jax.random.fold_in(stream_key, 6)
    for dim, parts in shards:
        steps = jnp.exp(jax.random.uniform(jax.random.fold_in(own, dim), (parts,), jnp.float32, low / len(shards), high / len(shards)))
        gain = gain * jnp.repeat(steps, dims[dim] // parts).reshape([-1 if axis == dim else 1 for axis in range(len(dims))])
    return gain


def centred(key, shape, spread, most, split=(), kind=jnp.bfloat16):
    result = spread * jax.random.normal(key, shape, jnp.float32)
    if split:
        result = result * block_scale(key, shape, split, -0.22, 0.18)
    return jnp.clip(result, -most, most).astype(kind)


def setup_inputs(seed: int = 0) -> dict:
    arg_keys = jax.random.split(jax.random.key(seed), 6)
    tokens = draw_tokens(jax.random.fold_in(arg_keys[5], 71), 0)
    slot_param = draw_slot_param(jax.random.fold_in(arg_keys[5], 71), 0)
    weight_in = centred(arg_keys[2], (EXPERTS, D, FF), D ** -0.5, 0.1875, ((0, 16), (2, 2)))
    weight_out = centred(arg_keys[3], (EXPERTS, FF, D), FF ** -0.5, 0.09375, ((0, 16), (1, 2)))
    grad_out = centred(arg_keys[4], (IMAGES, PATCHES, D), 1.0, 6.0, ((0, 32),))
    return dict(tokens=tokens, slot_param=slot_param, weight_in=weight_in, weight_out=weight_out, grad_out=grad_out)


def gelu_parts(pre):
    cdf = 0.5 * (1.0 + lax.erf(pre * 0.7071067811865476))
    slope = cdf + pre * jnp.exp(-0.5 * pre * pre) * 0.3989422804014327
    return pre * cdf, slope


def softmax_along(values, axis):
    top = jnp.max(values, axis=axis, keepdims=True)
    expo = jnp.exp(values - top)
    return expo / jnp.sum(expo, axis=axis, keepdims=True)


def expert_step(inputs):
    slot_x, slot_g, w_first, w_second = inputs
    pre = jnp.dot(slot_x, w_first, preferred_element_type=jnp.float32)
    value, slope = gelu_parts(pre)
    hidden = value.astype(jnp.bfloat16)
    slot_y = jnp.dot(hidden, w_second, preferred_element_type=jnp.float32).astype(jnp.bfloat16)
    back = jnp.dot(slot_g, w_second.T, preferred_element_type=jnp.float32)
    dpre = (back * slope).astype(jnp.bfloat16)
    grad_x = jnp.dot(dpre, w_first.T, preferred_element_type=jnp.float32).astype(jnp.bfloat16)
    grad_first = jnp.dot(slot_x.T, dpre, preferred_element_type=jnp.float32).astype(jnp.bfloat16)
    grad_second = jnp.dot(hidden.T, slot_g, preferred_element_type=jnp.float32).astype(jnp.bfloat16)
    return slot_y, grad_x, grad_first, grad_second


def reference(tokens, slot_param, weight_in, weight_out, grad_out):
    xf = tokens.astype(jnp.float32)
    gf = grad_out.astype(jnp.float32)
    pf = slot_param.astype(jnp.float32)
    logits = jnp.einsum('bpd,ds->bps', xf, pf)
    dispatch = softmax_along(logits, 1)
    combine = softmax_along(logits, 2)
    dispatch_b = dispatch.astype(jnp.bfloat16)
    combine_b = combine.astype(jnp.bfloat16)
    slot_in = jnp.einsum('bps,bpd->sbd', dispatch_b.astype(jnp.float32), xf).astype(jnp.bfloat16)
    slot_cot = jnp.einsum('bps,bpd->sbd', combine_b.astype(jnp.float32), gf).astype(jnp.bfloat16)
    slot_out, grad_slot, grad_win, grad_wout = lax.map(expert_step, (slot_in, slot_cot, weight_in, weight_out))
    d_combine = jnp.einsum('bpd,sbd->bps', gf, slot_out.astype(jnp.float32))
    d_dispatch = jnp.einsum('bpd,sbd->bps', xf, grad_slot.astype(jnp.float32))
    d_logits = dispatch * (d_dispatch - jnp.sum(dispatch * d_dispatch, axis=1, keepdims=True))
    d_logits = d_logits + combine * (d_combine - jnp.sum(combine * d_combine, axis=2, keepdims=True))
    d_logits = d_logits.astype(jnp.bfloat16).astype(jnp.float32)
    grad_tokens = jnp.einsum('bps,sbd->bpd', dispatch_b.astype(jnp.float32), grad_slot.astype(jnp.float32))
    grad_tokens = (grad_tokens + jnp.einsum('bps,ds->bpd', d_logits, pf)).astype(jnp.bfloat16)
    grad_param = jnp.einsum('bpd,bps->ds', xf, d_logits)
    return grad_tokens, grad_param, grad_win, grad_wout
```

```python
import jax
import jax.numpy as jnp
from jax import lax
from jax.sharding import PartitionSpec as P


def gelu_parts(pre):
    cdf = 0.5 * (1.0 + lax.erf(pre * 0.7071067811865476))
    slope = cdf + pre * jnp.exp(-0.5 * pre * pre) * 0.3989422804014327
    return (pre * cdf, slope)


def softmax_along(values, axis):
    top = jnp.max(values, axis=axis, keepdims=True)
    expo = jnp.exp(values - top)
    return expo / jnp.sum(expo, axis=axis, keepdims=True)


def swap(value, axis, mask):
    size = lax.axis_size(axis)
    return lax.ppermute(value, axis, [(k, k ^ mask) for k in range(size)])


def is_pow2(n):
    return n & (n - 1) == 0


def sum_bits(acc, axis, first_bit):
    size = lax.axis_size(axis)
    bit = first_bit
    while bit < size:
        sent = acc.astype(jnp.bfloat16)
        own = sent.astype(jnp.float32)
        if 2 * bit < size:
            a, b, c = (swap(sent, axis, m).astype(jnp.float32) for m in (bit, 2 * bit, 3 * bit))
            acc = (own + a) + (b + c)
            bit *= 4
        else:
            acc = own + swap(sent, axis, bit).astype(jnp.float32)
            bit *= 2
    return acc


def sum_everywhere(part):
    ex, ey = lax.axis_size("ex"), lax.axis_size("ey")
    if not (is_pow2(ex) and is_pow2(ey)) or ex < 2 or part.shape[0] % 2:
        return lax.psum(part, ("ex", "ey"))
    half = part.shape[0] // 2
    side = lax.axis_index("ex") % 2
    lo, hi = part[:half], part[half:]
    keep = jnp.where(side == 0, lo, hi).astype(jnp.bfloat16)
    give = jnp.where(side == 0, hi, lo).astype(jnp.bfloat16)
    acc = keep.astype(jnp.float32) + swap(give, "ex", 1).astype(jnp.float32)
    acc = sum_bits(acc, "ex", 2)
    acc = sum_bits(acc, "ey", 1)
    sent = acc.astype(jnp.bfloat16)
    own = sent.astype(jnp.float32)
    other = swap(sent, "ex", 1).astype(jnp.float32)
    return jnp.concatenate((jnp.where(side == 0, own, other), jnp.where(side == 0, other, own)), axis=0)


def gather_ex(value):
    if lax.axis_size("ex") == 2:
        other = swap(value, "ex", 1)
        side = lax.axis_index("ex")
        return jnp.concatenate(
            (jnp.where(side == 0, value, other), jnp.where(side == 0, other, value)), axis=0
        )
    return lax.all_gather(value, "ex", axis=0, tiled=True)


def scatter_sum_ex(value):
    if lax.axis_size("ex") == 2:
        side = lax.axis_index("ex")
        mine = jnp.where(side == 0, value[0], value[1])
        give = jnp.where(side == 0, value[1], value[0])
        got = swap(give.astype(jnp.bfloat16), "ex", 1)
        return (mine + got.astype(jnp.float32)).astype(jnp.bfloat16)
    return lax.psum_scatter(value.astype(jnp.bfloat16), "ex", scatter_dimension=0, tiled=True)[0]


def per_device(tokens, slot_param, weight_in, weight_out, grad_out):
    ex, ey = lax.axis_size("ex"), lax.axis_size("ey")
    images, _, width = tokens.shape
    slots = slot_param.shape[1]
    mine = slots // ey
    logits = jnp.einsum("ipd,ds->ips", tokens, slot_param, preferred_element_type=jnp.float32)
    dispatch = softmax_along(logits, 1)
    combine = softmax_along(logits, 2)
    dispatch_b = dispatch.astype(jnp.bfloat16)
    combine_b = combine.astype(jnp.bfloat16)
    slot_in = jnp.einsum(
        "ips,ipd->isd", dispatch_b, tokens, preferred_element_type=jnp.float32
    ).astype(jnp.bfloat16)
    slot_cot = jnp.einsum(
        "ips,ipd->isd", combine_b, grad_out, preferred_element_type=jnp.float32
    ).astype(jnp.bfloat16)
    stacked = jnp.stack((slot_in, slot_cot), axis=1)
    moved = lax.all_to_all(stacked, "ey", split_axis=2, concat_axis=0, tiled=True)
    arrived = gather_ex(moved)
    rows = arrived.shape[0]
    slot_x = arrived[:, 0]
    slot_g = arrived[:, 1]
    pre = jnp.einsum("red,edf->ref", slot_x, weight_in, preferred_element_type=jnp.float32)
    value, slope = gelu_parts(pre)
    hidden = value.astype(jnp.bfloat16)
    back = jnp.einsum("red,efd->ref", slot_g, weight_out, preferred_element_type=jnp.float32)
    dpre = (back * slope).astype(jnp.bfloat16)
    part_out = jnp.einsum("ref,efd->red", hidden, weight_out, preferred_element_type=jnp.float32)
    part_grad = jnp.einsum("ref,edf->red", dpre, weight_in, preferred_element_type=jnp.float32)
    paired = jnp.stack((part_out, part_grad), axis=1)
    summed = scatter_sum_ex(paired.reshape((ex, rows // ex) + paired.shape[1:]))
    paired = lax.all_to_all(summed, "ey", split_axis=0, concat_axis=2, tiled=True)
    slot_out = paired[:, 0]
    grad_slot = paired[:, 1]
    grad_win = jnp.einsum("red,ref->edf", slot_x, dpre, preferred_element_type=jnp.float32).astype(
        jnp.bfloat16
    )
    grad_wout = jnp.einsum(
        "ref,red->efd", hidden, slot_g, preferred_element_type=jnp.float32
    ).astype(jnp.bfloat16)
    d_combine = jnp.einsum("ipd,isd->ips", grad_out, slot_out, preferred_element_type=jnp.float32)
    d_dispatch = jnp.einsum("ipd,isd->ips", tokens, grad_slot, preferred_element_type=jnp.float32)
    d_logits = dispatch * (d_dispatch - jnp.sum(dispatch * d_dispatch, axis=1, keepdims=True))
    d_logits = d_logits + combine * (
        d_combine - jnp.sum(combine * d_combine, axis=2, keepdims=True)
    )
    logit_grad = d_logits.astype(jnp.bfloat16)
    local_param = jnp.einsum("ipd,ips->ds", tokens, logit_grad, preferred_element_type=jnp.float32)
    grad_param = sum_everywhere(local_param)
    grad_tokens = jnp.einsum(
        "ips,isd->ipd", dispatch_b, grad_slot, preferred_element_type=jnp.float32
    )
    grad_tokens = grad_tokens + jnp.einsum(
        "ips,ds->ipd", logit_grad, slot_param, preferred_element_type=jnp.float32
    )
    return (grad_tokens.astype(jnp.bfloat16), grad_param, grad_win, grad_wout)


def solution(mesh):
    in_specs = (
        P(("ex", "ey"), None, None),
        P(),
        P("ey", None, "ex"),
        P("ey", "ex", None),
        P(("ex", "ey"), None, None),
    )
    out_specs = (P(("ex", "ey"), None, None), P(), P("ey", None, "ex"), P("ey", "ex", None))
    return jax.shard_map(
        per_device, mesh=mesh, in_specs=in_specs, out_specs=out_specs, check_vma=False
    )
```

```python
import jax
import jax.numpy as jnp
from jax import lax
from jax.experimental import pallas as pl
from jax.experimental.pallas import tpu as pltpu
from jax.sharding import PartitionSpec as P


def gelu_parts(pre):
    cdf = 0.5 * (1.0 + lax.erf(pre * 0.7071067811865476))
    slope = cdf + pre * jnp.exp(-0.5 * pre * pre) * 0.3989422804014327
    return (pre * cdf, slope)


def softmax_along(values, axis):
    top = jnp.max(values, axis=axis, keepdims=True)
    expo = jnp.exp(values - top)
    return expo / jnp.sum(expo, axis=axis, keepdims=True)


def dot(a, b, contract):
    return lax.dot_general(a, b, (contract, ((), ())), preferred_element_type=jnp.float32)


def in_hbm(value):
    return pltpu.with_memory_space_constraint(value, pltpu.HBM)


NN, NT, TN = ((1,), (0,)), ((1,), (1,)), ((0,), (0,))


def spread(rows, slots, mine, kind):
    row = lax.broadcasted_iota(jnp.int32, (rows, slots), 0)
    slot = lax.broadcasted_iota(jnp.int32, (rows, slots), 1)
    target = (slot // mine) * (2 * mine) + kind * mine + slot % mine
    return jnp.where(row == target, 1.0, 0.0).astype(jnp.bfloat16)


def route_kernel(mine, tok_ref, out_ref, par_ref, sent_ref, disp_ref, comb_ref):
    tok = tok_ref[0]
    slots = par_ref.shape[0]
    logits = dot(par_ref[...], tok, NT)
    dispatch = softmax_along(logits, 1)
    combine = softmax_along(logits, 0)
    disp_ref[0] = dispatch
    comb_ref[0] = combine
    first = dot(spread(2 * slots, slots, mine, 0), dispatch.astype(jnp.bfloat16), NN)
    second = dot(spread(2 * slots, slots, mine, 1), combine.astype(jnp.bfloat16), NN)
    both = dot(first.astype(jnp.bfloat16), tok, NN) + dot(second.astype(jnp.bfloat16), out_ref[0], NN)
    for k in range(slots // mine):
        sent_ref[k, 0] = both[2 * mine * k : 2 * mine * (k + 1)].astype(jnp.bfloat16)


def route_forward(tokens, grad_out, param_t, owners):
    images, patches, width = tokens.shape
    slots = param_t.shape[0]
    mine = slots // owners
    whole = pl.BlockSpec((1, patches, width), lambda i: (i, 0, 0))
    table = pl.BlockSpec((1, slots, patches), lambda i: (i, 0, 0))
    return pl.pallas_call(
        lambda *refs: route_kernel(mine, *refs),
        grid=(images,),
        in_specs=[whole, whole, pl.BlockSpec((slots, width), lambda i: (0, 0))],
        out_specs=[pl.BlockSpec((owners, 1, 2 * mine, width), lambda i: (0, i, 0, 0)), table, table],
        out_shape=[
            jax.ShapeDtypeStruct((owners, images, 2 * mine, width), jnp.bfloat16),
            jax.ShapeDtypeStruct((images, slots, patches), jnp.float32),
            jax.ShapeDtypeStruct((images, slots, patches), jnp.float32),
        ],
        compiler_params=pltpu.CompilerParams(vmem_limit_bytes=16 << 20),
        name="route_forward",
    )(in_hbm(tokens), in_hbm(grad_out), in_hbm(param_t))


def expert_body(experts, chunks, x_ref, win_hbm, wout_hbm, part_ref, hid_ref, dpre_ref, win_v, wout_v, sems):
    step = win_v.shape[2] // chunks
    order = [(e, c) for e in range(experts) for c in range(chunks)]

    def copies(e, c):
        cols = pl.ds(c * step, step)
        return (
            pltpu.make_async_copy(win_hbm.at[e, :, cols], win_v.at[e, :, cols], sems.at[0, e, c]),
            pltpu.make_async_copy(wout_hbm.at[e, cols, :], wout_v.at[e, cols, :], sems.at[1, e, c]),
        )

    def open_chunk(e, c):
        for copy in copies(e, c):
            copy.wait()
        cols = pl.ds(c * step, step)
        return dot(x_ref[e], win_v[e, :, cols], NN), dot(x_ref[experts + e], wout_v[e, cols, :], NT)

    for e, c in order:
        for copy in copies(e, c):
            copy.start()
    ready = open_chunk(*order[0])
    out = grad = None
    for k, (e, c) in enumerate(order):
        pre, back = ready
        if k + 1 < len(order):
            ready = open_chunk(*order[k + 1])
        cols = pl.ds(c * step, step)
        value, slope = gelu_parts(pre)
        hidden = value.astype(jnp.bfloat16)
        dpre = (back * slope).astype(jnp.bfloat16)
        hid_ref[e, :, cols] = hidden
        dpre_ref[e, :, cols] = dpre
        o = dot(hidden, wout_v[e, cols, :], NN)
        d = dot(dpre, win_v[e, :, cols], NT)
        out, grad = (o, d) if c == 0 else (out + o, grad + d)
        if c == chunks - 1:
            part_ref[e] = out
            part_ref[experts + e] = grad


def chunk_count(size, wanted):
    while size % wanted or (size // wanted) % 128 and wanted > 1:
        wanted -= 1
    return wanted


def expert_forward(rows_in, weight_in, weight_out):
    experts, width, hid = weight_in.shape
    rows = rows_in.shape[1]
    chunks = chunk_count(hid, 4)
    vmem = pl.BlockSpec(memory_space=pltpu.VMEM)
    hbm = pl.BlockSpec(memory_space=pl.ANY)
    return pl.pallas_call(
        lambda *refs: expert_body(experts, chunks, *refs),
        in_specs=[vmem, hbm, hbm],
        out_specs=[vmem, vmem, vmem],
        out_shape=[
            jax.ShapeDtypeStruct((2 * experts, rows, width), jnp.float32),
            jax.ShapeDtypeStruct((experts, rows, hid), jnp.bfloat16),
            jax.ShapeDtypeStruct((experts, rows, hid), jnp.bfloat16),
        ],
        scratch_shapes=[
            pltpu.VMEM((experts, width, hid), jnp.bfloat16),
            pltpu.VMEM((experts, hid, width), jnp.bfloat16),
            pltpu.SemaphoreType.DMA((2, experts, chunks)),
        ],
        compiler_params=pltpu.CompilerParams(vmem_limit_bytes=22 << 20),
        name="expert_forward",
    )(rows_in, in_hbm(weight_in), in_hbm(weight_out))


def weight_grad_kernel(x_ref, g_ref, hid_ref, dpre_ref, gin_ref, gout_ref):
    gin_ref[0] = dot(x_ref[0], dpre_ref[0], TN).astype(jnp.bfloat16)
    gout_ref[0] = dot(hid_ref[0], g_ref[0], TN).astype(jnp.bfloat16)


def weight_grads(rows_in, hidden, dpre):
    experts, rows, hid = hidden.shape
    width = rows_in.shape[2]
    chunks = chunk_count(hid, 4)
    step = hid // chunks
    return pl.pallas_call(
        weight_grad_kernel,
        grid=(experts, chunks),
        in_specs=[
            pl.BlockSpec((1, rows, width), lambda e, c: (e, 0, 0)),
            pl.BlockSpec((1, rows, width), lambda e, c: (experts + e, 0, 0)),
            pl.BlockSpec((1, rows, step), lambda e, c: (e, 0, c)),
            pl.BlockSpec((1, rows, step), lambda e, c: (e, 0, c)),
        ],
        out_specs=[
            pl.BlockSpec((1, width, step), lambda e, c: (e, 0, c)),
            pl.BlockSpec((1, step, width), lambda e, c: (e, c, 0)),
        ],
        out_shape=[
            jax.ShapeDtypeStruct((experts, width, hid), jnp.bfloat16),
            jax.ShapeDtypeStruct((experts, hid, width), jnp.bfloat16),
        ],
        compiler_params=pltpu.CompilerParams(vmem_limit_bytes=24 << 20),
        name="weight_grads",
    )(rows_in, rows_in, hidden, dpre)


def swap(value, axis, mask):
    size = lax.axis_size(axis)
    return lax.ppermute(value, axis, [(k, k ^ mask) for k in range(size)])


def is_pow2(n):
    return n & (n - 1) == 0


def sum_bits(acc, axis, first_bit):
    size = lax.axis_size(axis)
    bit = first_bit
    while bit < size:
        sent = acc.astype(jnp.bfloat16)
        own = sent.astype(jnp.float32)
        if 2 * bit < size:
            a, b, c = (swap(sent, axis, m).astype(jnp.float32) for m in (bit, 2 * bit, 3 * bit))
            acc = (own + a) + (b + c)
            bit *= 4
        else:
            acc = own + swap(sent, axis, bit).astype(jnp.float32)
            bit *= 2
    return acc


def sum_everywhere(part):
    ex, ey = lax.axis_size("ex"), lax.axis_size("ey")
    if not (is_pow2(ex) and is_pow2(ey)) or ex < 2 or part.shape[0] % 2:
        return lax.psum(part, ("ex", "ey"))
    half = part.shape[0] // 2
    side = lax.axis_index("ex") % 2
    lo, hi = part[:half], part[half:]
    keep = jnp.where(side == 0, lo, hi).astype(jnp.bfloat16)
    give = jnp.where(side == 0, hi, lo).astype(jnp.bfloat16)
    acc = keep.astype(jnp.float32) + swap(give, "ex", 1).astype(jnp.float32)
    acc = sum_bits(acc, "ex", 2)
    acc = sum_bits(acc, "ey", 1)
    sent = acc.astype(jnp.bfloat16)
    own = sent.astype(jnp.float32)
    other = swap(sent, "ex", 1).astype(jnp.float32)
    return jnp.concatenate((jnp.where(side == 0, own, other), jnp.where(side == 0, other, own)), axis=0)


def gather_ex(value):
    if lax.axis_size("ex") == 2:
        return jnp.stack((value, swap(value, "ex", 1)))
    return lax.all_gather(value, "ex", axis=0)


def scatter_sum_ex(parts):
    if lax.axis_size("ex") == 2:
        got = swap(parts[1].astype(jnp.bfloat16), "ex", 1)
        return (parts[0] + got.astype(jnp.float32)).astype(jnp.bfloat16)
    return lax.psum_scatter(parts.astype(jnp.bfloat16), "ex", scatter_dimension=0)


def per_device(tokens, slot_param, weight_in, weight_out, grad_out):
    ex, ey = lax.axis_size("ex"), lax.axis_size("ey")
    images, _, width = tokens.shape
    slots = slot_param.shape[1]
    mine = slots // ey
    param_t = slot_param.T
    sent, dispatch, combine = route_forward(tokens, grad_out, param_t, ey)
    moved = lax.all_to_all(sent.reshape(ey * images, 2 * mine, width), "ey", split_axis=0, concat_axis=0, tiled=True)
    arrived = gather_ex(moved)
    rows = ex * ey * images
    rows_in = arrived.reshape(rows, 2 * mine, width).transpose(1, 0, 2)
    parts, hidden, dpre = expert_forward(rows_in, weight_in, weight_out)
    summed = scatter_sum_ex(parts.transpose(1, 0, 2).reshape(ex, ey * images, 2 * mine, width))
    back = lax.all_to_all(summed, "ey", split_axis=0, concat_axis=0, tiled=True)
    grad_win, grad_wout = weight_grads(rows_in, hidden, dpre)
    back = back.reshape(ey, images, 2, mine, width).transpose(1, 2, 0, 3, 4).reshape(images, 2, slots, width)
    slot_out = back[:, 0]
    grad_slot = back[:, 1]
    d_combine = jnp.einsum("isd,ipd->isp", slot_out, grad_out, preferred_element_type=jnp.float32)
    d_dispatch = jnp.einsum("isd,ipd->isp", grad_slot, tokens, preferred_element_type=jnp.float32)
    d_logits = dispatch * (d_dispatch - jnp.sum(dispatch * d_dispatch, axis=2, keepdims=True))
    d_logits = d_logits + combine * (
        d_combine - jnp.sum(combine * d_combine, axis=1, keepdims=True)
    )
    logit_grad = d_logits.astype(jnp.bfloat16)
    local_param = jnp.einsum("isp,ipd->sd", logit_grad, tokens, preferred_element_type=jnp.float32)
    grad_param = sum_everywhere(local_param).T
    grad_tokens = jnp.einsum(
        "isp,isd->ipd", dispatch.astype(jnp.bfloat16), grad_slot, preferred_element_type=jnp.float32
    )
    grad_tokens = grad_tokens + jnp.einsum(
        "isp,sd->ipd", logit_grad, param_t, preferred_element_type=jnp.float32
    )
    return (grad_tokens.astype(jnp.bfloat16), grad_param, grad_win, grad_wout)


def solution(mesh):
    in_specs = (
        P(("ex", "ey"), None, None),
        P(),
        P("ey", None, "ex"),
        P("ey", "ex", None),
        P(("ex", "ey"), None, None),
    )
    out_specs = (P(("ex", "ey"), None, None), P(), P("ey", None, "ex"), P("ey", "ex", None))

    return jax.shard_map(per_device, mesh=mesh, in_specs=in_specs, out_specs=out_specs, check_vma=False)
```

```python
import jax
import jax.numpy as jnp
from jax import lax
from jax.experimental import pallas as pl
from jax.experimental.pallas import tpu as pltpu
from jax.sharding import PartitionSpec as P


def gelu_parts(pre):
    cdf = 0.5 * (1.0 + lax.erf(pre * 0.7071067811865476))
    slope = cdf + pre * jnp.exp(-0.5 * pre * pre) * 0.3989422804014327
    return (pre * cdf, slope)


def softmax_along(values, axis):
    top = jnp.max(values, axis=axis, keepdims=True)
    expo = jnp.exp(values - top)
    return expo / jnp.sum(expo, axis=axis, keepdims=True)


def dot(a, b, contract):
    return lax.dot_general(a, b, (contract, ((), ())), preferred_element_type=jnp.float32)


def in_hbm(value):
    return pltpu.with_memory_space_constraint(value, pltpu.HBM)


NN, NT, TN = ((1,), (0,)), ((1,), (1,)), ((0,), (0,))


def chunk_count(size, wanted):
    while size % wanted or (size // wanted) % 256 and wanted > 1:
        wanted -= 1
    return wanted


CHUNKS, AHEAD, FLIGHT = 8, 3, 4


def first_columns(hid):
    chunks = chunk_count(hid, CHUNKS)
    return min(AHEAD, chunks) * (hid // chunks)


def row_kind(shape, mine):
    return (lax.broadcasted_iota(jnp.int32, shape, 0) // mine) % 2


def slot_rows(slots, mine, wide, kind=None):
    shape = (2 * slots, slots) if wide else (slots, 2 * slots)
    row = lax.broadcasted_iota(jnp.int32, shape, 0 if wide else 1)
    slot = lax.broadcasted_iota(jnp.int32, shape, 1 if wide else 0)
    hit = (row // (2 * mine)) * mine + row % mine == slot
    if kind is not None:
        hit = hit & ((row // mine) % 2 == kind)
    return jnp.where(hit, 1.0, 0.0).astype(jnp.bfloat16)


def route_kernel(
    mine, tok_hbm, out_hbm, par_hbm, win_hbm, wout_hbm,
    sent_ref, mix_ref, win_v, wout_v, tok_v, out_v, par_v, sems,
):
    slots, first = par_v.shape[0], win_v.shape[1]
    loads = [
        pltpu.make_async_copy(par_hbm, par_v, sems.at[0]),
        pltpu.make_async_copy(tok_hbm, tok_v, sems.at[1]),
        pltpu.make_async_copy(out_hbm, out_v, sems.at[2]),
        pltpu.make_async_copy(win_hbm.at[0, :, pl.ds(0, first)], win_v, sems.at[3]),
        pltpu.make_async_copy(wout_hbm.at[0, pl.ds(0, first), :], wout_v, sems.at[4]),
    ]
    for load in loads:
        load.start()
    loads[0].wait()
    par = dot(slot_rows(slots, mine, True), par_v[...], NN).astype(jnp.bfloat16)
    loads[1].wait()
    for image in range(tok_v.shape[0]):
        tok = tok_v[image]
        logits = dot(par, tok, NT)
        dispatch = softmax_along(logits, 1)
        expo = jnp.exp(logits - jnp.max(logits, axis=0, keepdims=True))
        combine = expo / (0.5 * jnp.sum(expo, axis=0, keepdims=True))
        is_in = row_kind(logits.shape, mine) == 0
        mix_ref[image] = jnp.where(is_in, dispatch, combine)
        left = jnp.where(is_in, dispatch, 0.0).astype(jnp.bfloat16)
        right = jnp.where(is_in, 0.0, combine).astype(jnp.bfloat16)
        both = dot(left, tok, NN)
        if image == 0:
            loads[2].wait()
        both = both + dot(right, out_v[image], NN)
        for k in range(slots // mine):
            sent_ref[k, image] = both[2 * mine * k : 2 * mine * (k + 1)].astype(jnp.bfloat16)
    loads[3].wait()
    loads[4].wait()


def route_forward(tokens, grad_out, param_t, weight_in, weight_out, owners):
    images, patches, width = tokens.shape
    slots = param_t.shape[0]
    mine = slots // owners
    first = first_columns(weight_in.shape[2])
    vmem = pl.BlockSpec(memory_space=pltpu.VMEM)
    hbm = pl.BlockSpec(memory_space=pl.ANY)
    return pl.pallas_call(
        lambda *refs: route_kernel(mine, *refs),
        in_specs=[hbm] * 5,
        out_specs=[vmem] * 4,
        out_shape=[
            jax.ShapeDtypeStruct((owners, images, 2 * mine, width), jnp.bfloat16),
            jax.ShapeDtypeStruct((images, 2 * slots, patches), jnp.float32),
            jax.ShapeDtypeStruct((width, first), jnp.bfloat16),
            jax.ShapeDtypeStruct((first, width), jnp.bfloat16),
        ],
        scratch_shapes=[
            pltpu.VMEM(tokens.shape, jnp.bfloat16),
            pltpu.VMEM(grad_out.shape, jnp.bfloat16),
            pltpu.VMEM(param_t.shape, jnp.bfloat16),
            pltpu.SemaphoreType.DMA((5,)),
        ],
        compiler_params=pltpu.CompilerParams(vmem_limit_bytes=16 << 20),
        name="route_forward",
    )(in_hbm(tokens), in_hbm(grad_out), in_hbm(param_t), in_hbm(weight_in), in_hbm(weight_out))


def route_back_kernel(mine, side_ref, back_ref, mix_ref, tok_ref, out_ref, rows_ref, dl_ref, keep_ref, give_ref, raw, part):
    slots = dl_ref.shape[1]
    total = None
    for image in range(tok_ref.shape[0]):
        for k in range(slots // mine):
            raw[2 * mine * k : 2 * mine * (k + 1), :] = back_ref[k, image].astype(jnp.float32)
        rows = raw[...].astype(jnp.bfloat16)
        rows_ref[image] = rows
        tok = tok_ref[image]
        mix = mix_ref[image]
        is_in = row_kind(mix.shape, mine) == 0
        d = jnp.where(is_in, dot(rows, tok, NT), dot(rows, out_ref[image], NT))
        weighed = mix * d
        over_patches = jnp.sum(weighed, axis=1, keepdims=True)
        over_slots = jnp.sum(jnp.where(is_in, 0.0, weighed), axis=0, keepdims=True)
        term = mix * (d - jnp.where(is_in, over_patches, over_slots))
        pair = (term + pltpu.roll(term, 2 * slots - mine, 0)).astype(jnp.bfloat16)
        dl = dot(slot_rows(slots, mine, False, 0), pair, NN).astype(jnp.bfloat16)
        dl_ref[image] = dl
        local = dot(dl, tok, NN)
        total = local if total is None else total + local
    half = slots // 2
    part[...] = total
    side = side_ref[0]
    keep_ref[...] = part[pl.ds(pl.multiple_of(side * half, half), half), :].astype(jnp.bfloat16)
    give_ref[...] = part[pl.ds(pl.multiple_of((1 - side) * half, half), half), :].astype(jnp.bfloat16)


def route_back(side, back, mix, tokens, grad_out):
    owners, images, block, width = back.shape
    mine = block // 2
    slots = owners * mine
    vmem = pl.BlockSpec(memory_space=pltpu.VMEM)
    return pl.pallas_call(
        lambda *refs: route_back_kernel(mine, *refs),
        in_specs=[pl.BlockSpec(memory_space=pltpu.SMEM)] + [vmem] * 4,
        out_specs=[vmem] * 4,
        out_shape=[
            jax.ShapeDtypeStruct((images, 2 * slots, width), jnp.bfloat16),
            jax.ShapeDtypeStruct((images, slots, tokens.shape[1]), jnp.bfloat16),
            jax.ShapeDtypeStruct((slots // 2, width), jnp.bfloat16),
            jax.ShapeDtypeStruct((slots // 2, width), jnp.bfloat16),
        ],
        scratch_shapes=[
            pltpu.VMEM((2 * slots, width), jnp.float32),
            pltpu.VMEM((slots, width), jnp.float32),
        ],
        compiler_params=pltpu.CompilerParams(vmem_limit_bytes=16 << 20),
        name="route_back",
    )(side, back, mix, tokens, grad_out)


def token_grad_kernel(mine, mix_ref, rows_ref, dl_ref, par_ref, grad_ref):
    mix = mix_ref[0]
    left = jnp.where(row_kind(mix.shape, mine) == 0, mix, 0.0).astype(jnp.bfloat16)
    grad_ref[0] = (dot(left, rows_ref[0], TN) + dot(dl_ref[0], par_ref[...], TN)).astype(jnp.bfloat16)


def token_grads(mine, mix, rows, dl, param_t):
    images, twice, patches = mix.shape
    slots, width = param_t.shape
    return pl.pallas_call(
        lambda *refs: token_grad_kernel(mine, *refs),
        grid=(images,),
        in_specs=[
            pl.BlockSpec((1, twice, patches), lambda i: (i, 0, 0)),
            pl.BlockSpec((1, twice, width), lambda i: (i, 0, 0)),
            pl.BlockSpec((1, slots, patches), lambda i: (i, 0, 0)),
            pl.BlockSpec((slots, width), lambda i: (0, 0)),
        ],
        out_specs=pl.BlockSpec((1, patches, width), lambda i: (i, 0, 0)),
        out_shape=jax.ShapeDtypeStruct((images, patches, width), jnp.bfloat16),
        compiler_params=pltpu.CompilerParams(vmem_limit_bytes=16 << 20),
        name="token_grads",
    )(mix, rows, dl, param_t)


def expert_body(
    experts, chunks, x_ref, first_in, first_out, win_hbm, wout_hbm,
    part_ref, give_ref, hid_ref, dpre_ref, win_v, wout_v, sems,
):
    own = part_ref.shape[1]
    step = win_v.shape[2] // chunks
    order = [(e, c) for e in range(experts) for c in range(chunks)]
    held = first_in.shape[1] // step

    def copies(k):
        e, c = order[k]
        cols = pl.ds(c * step, step)
        return (
            pltpu.make_async_copy(win_hbm.at[e, :, cols], win_v.at[e, :, cols], sems.at[0, e, c]),
            pltpu.make_async_copy(wout_hbm.at[e, cols, :], wout_v.at[e, cols, :], sems.at[1, e, c]),
        )

    def start(k):
        if k < len(order):
            for copy in copies(k):
                copy.start()

    def weights(k):
        e, c = order[k]
        cols = pl.ds(c * step, step)
        if k < held:
            return first_in.at[:, cols], first_out.at[cols, :]
        return win_v.at[e, :, cols], wout_v.at[e, cols, :]

    groups = {held: 1}
    k = held + 1
    while k < len(order):
        groups[k] = min(2, len(order) - k)
        k += groups[k]

    for k in range(held, held + FLIGHT):
        start(k)
    ready = out = grad = None
    for k in range(len(order) + 1):
        for arriving in range(k, k + groups.get(k, 0)):
            if arriving < len(order):
                for copy in copies(arriving):
                    copy.wait()
                start(arriving + FLIGHT)
        before = ready
        if k < len(order):
            w1, w2 = weights(k)
            e = order[k][0]
            ready = dot(x_ref[e], w1[...], NN), dot(x_ref[experts + e], w2[...], NT)
        if before is None:
            continue
        e, c = order[k - 1]
        w1, w2 = weights(k - 1)
        cols = pl.ds(c * step, step)
        pre, back = before
        value, slope = gelu_parts(pre)
        hidden = value.astype(jnp.bfloat16)
        dpre = (back * slope).astype(jnp.bfloat16)
        hid_ref[e, :, cols] = hidden
        dpre_ref[e, :, cols] = dpre
        o = dot(hidden, w2[...], NN)
        d = dot(dpre, w1[...], NT)
        out, grad = (o, d) if c == 0 else (out + o, grad + d)
        if c == chunks - 1:
            part_ref[e] = grad[:own]
            part_ref[experts + e] = out[:own]
            if own < out.shape[0]:
                give_ref[e] = grad[own:].astype(jnp.bfloat16)
                give_ref[experts + e] = out[own:].astype(jnp.bfloat16)
            else:
                give_ref[...] = jnp.zeros_like(give_ref)


def expert_forward(rows_in, first_in, first_out, weight_in, weight_out, own):
    experts, width, hid = weight_in.shape
    rows = rows_in.shape[1]
    chunks = chunk_count(hid, CHUNKS)
    vmem = pl.BlockSpec(memory_space=pltpu.VMEM)
    hbm = pl.BlockSpec(memory_space=pl.ANY)
    return pl.pallas_call(
        lambda *refs: expert_body(experts, chunks, *refs),
        in_specs=[vmem, vmem, vmem, hbm, hbm],
        out_specs=[vmem, vmem, vmem, vmem],
        out_shape=[
            jax.ShapeDtypeStruct((2 * experts, own, width), jnp.float32),
            jax.ShapeDtypeStruct((2 * experts, max(rows - own, 8), width), jnp.bfloat16),
            jax.ShapeDtypeStruct((experts, rows, hid), jnp.bfloat16),
            jax.ShapeDtypeStruct((experts, rows, hid), jnp.bfloat16),
        ],
        scratch_shapes=[
            pltpu.VMEM((experts, width, hid), jnp.bfloat16),
            pltpu.VMEM((experts, hid, width), jnp.bfloat16),
            pltpu.SemaphoreType.DMA((2, experts, chunks)),
        ],
        compiler_params=pltpu.CompilerParams(vmem_limit_bytes=22 << 20),
        name="expert_forward",
    )(rows_in, first_in, first_out, in_hbm(weight_in), in_hbm(weight_out))


def weight_grad_kernel(x_ref, g_ref, hid_ref, dpre_ref, gin_ref, gout_ref):
    gin_ref[0] = dot(x_ref[0], dpre_ref[0], TN).astype(jnp.bfloat16)
    gout_ref[0] = dot(hid_ref[0], g_ref[0], TN).astype(jnp.bfloat16)


def weight_grads(rows_in, hidden, dpre):
    experts, rows, hid = hidden.shape
    width = rows_in.shape[2]
    chunks = chunk_count(hid, 4)
    step = hid // chunks
    return pl.pallas_call(
        weight_grad_kernel,
        grid=(experts, chunks),
        in_specs=[
            pl.BlockSpec((1, rows, width), lambda e, c: (e, 0, 0)),
            pl.BlockSpec((1, rows, width), lambda e, c: (experts + e, 0, 0)),
            pl.BlockSpec((1, rows, step), lambda e, c: (e, 0, c)),
            pl.BlockSpec((1, rows, step), lambda e, c: (e, 0, c)),
        ],
        out_specs=[
            pl.BlockSpec((1, width, step), lambda e, c: (e, 0, c)),
            pl.BlockSpec((1, step, width), lambda e, c: (e, c, 0)),
        ],
        out_shape=[
            jax.ShapeDtypeStruct((experts, width, hid), jnp.bfloat16),
            jax.ShapeDtypeStruct((experts, hid, width), jnp.bfloat16),
        ],
        compiler_params=pltpu.CompilerParams(vmem_limit_bytes=24 << 20),
        name="weight_grads",
    )(rows_in, rows_in, hidden, dpre)


def swap(value, axis, mask):
    size = lax.axis_size(axis)
    return lax.ppermute(value, axis, [(k, k ^ mask) for k in range(size)])


def is_pow2(n):
    return n & (n - 1) == 0


def sum_bits(acc, axis, first_bit):
    size = lax.axis_size(axis)
    bit = first_bit
    while bit < size:
        sent = acc.astype(jnp.bfloat16)
        own = sent.astype(jnp.float32)
        if 2 * bit < size:
            a, b, c = (swap(sent, axis, m).astype(jnp.float32) for m in (bit, 2 * bit, 3 * bit))
            acc = (own + a) + (b + c)
            bit *= 4
        else:
            acc = own + swap(sent, axis, bit).astype(jnp.float32)
            bit *= 2
    return acc


def sum_everywhere(keep, give, side):
    ex, ey = lax.axis_size("ex"), lax.axis_size("ey")
    if not (is_pow2(ex) and is_pow2(ey)):
        low = jnp.where(side == 0, keep, give).astype(jnp.float32)
        high = jnp.where(side == 0, give, keep).astype(jnp.float32)
        return lax.psum(jnp.concatenate((low, high), axis=0), ("ex", "ey"))
    acc = keep.astype(jnp.float32) + swap(give, "ex", 1).astype(jnp.float32)
    acc = sum_bits(acc, "ex", 2)
    acc = sum_bits(acc, "ey", 1)
    sent = acc.astype(jnp.bfloat16)
    own = sent.astype(jnp.float32)
    other = swap(sent, "ex", 1)
    other = other.astype(jnp.float32)
    return jnp.concatenate((jnp.where(side == 0, own, other), jnp.where(side == 0, other, own)), axis=0)


def gather_ex(value):
    if lax.axis_size("ex") == 2:
        return jnp.stack((value, swap(value, "ex", 1)))
    return lax.all_gather(value, "ex", axis=0)


def join_kernel(keep_ref, got_ref, sum_hbm, sum_v, sem):
    block, rows, width = keep_ref.shape
    total = (keep_ref[...] + got_ref[...].astype(jnp.float32)).reshape(block * rows, width)
    shape = (block * rows, block * rows)
    to = lax.broadcasted_iota(jnp.int32, shape, 0)
    at = lax.broadcasted_iota(jnp.int32, shape, 1)
    move = jnp.where((to % block) * rows + to // block == at, 1.0, 0.0).astype(jnp.bfloat16)
    moved = dot(move, total.astype(jnp.bfloat16), NN)
    for k in range(rows):
        sum_v[k] = moved[block * k : block * (k + 1)].astype(jnp.bfloat16)
    copy = pltpu.make_async_copy(sum_v, sum_hbm, sem)
    copy.start()
    copy.wait()


def join(keep, got):
    block, rows, width = keep.shape
    vmem = pl.BlockSpec(memory_space=pltpu.VMEM)
    return pl.pallas_call(
        lambda *refs: join_kernel(*refs),
        in_specs=[vmem, vmem],
        out_specs=pl.BlockSpec(memory_space=pl.ANY),
        out_shape=pltpu.HBM((rows, block, width), jnp.bfloat16),
        scratch_shapes=[pltpu.VMEM((rows, block, width), jnp.bfloat16), pltpu.SemaphoreType.DMA],
        compiler_params=pltpu.CompilerParams(vmem_limit_bytes=16 << 20),
        name="join",
    )(keep, got)


def per_device(tokens, slot_param, weight_in, weight_out, grad_out):
    ex, ey = lax.axis_size("ex"), lax.axis_size("ey")
    images, _, width = tokens.shape
    slots = slot_param.shape[1]
    mine = slots // ey
    param_t = slot_param.T
    sent, mix, first_in, first_out = route_forward(tokens, grad_out, param_t, weight_in, weight_out, ey)
    moved = lax.all_to_all(sent.reshape(ey * images, 2 * mine, width), "ey", split_axis=0, concat_axis=0, tiled=True)
    arrived = gather_ex(moved)
    rows = ex * ey * images
    rows_in = arrived.reshape(rows, 2 * mine, width).transpose(1, 0, 2)
    own = rows // 2 if ex == 2 else rows
    keep_rows, give_rows, hidden, dpre = expert_forward(
        rows_in, first_in, first_out, weight_in, weight_out, own
    )
    if ex == 2:
        summed = join(keep_rows, swap(give_rows, "ex", 1))
    else:
        blocks = keep_rows.astype(jnp.bfloat16).transpose(1, 0, 2).reshape(ex, ey * images, 2 * mine, width)
        summed = lax.psum_scatter(blocks, "ex", scatter_dimension=0)
    back = lax.all_to_all(summed, "ey", split_axis=0, concat_axis=0, tiled=True)
    grad_win, grad_wout = weight_grads(rows_in, hidden, dpre)
    side = lax.axis_index("ex") % 2
    back_rows, logit_grad, keep, give = route_back(
        side.reshape(1), back.reshape(ey, images, 2 * mine, width), mix, tokens, grad_out
    )
    grad_param = sum_everywhere(keep, give, side).T
    grad_tokens = token_grads(mine, mix, back_rows, logit_grad, param_t)
    return (grad_tokens, grad_param, grad_win, grad_wout)


def solution(mesh):
    in_specs = (
        P(("ex", "ey"), None, None),
        P(),
        P("ey", None, "ex"),
        P("ey", "ex", None),
        P(("ex", "ey"), None, None),
    )
    out_specs = (P(("ex", "ey"), None, None), P(), P("ey", None, "ex"), P("ey", "ex", None))

    return jax.shard_map(per_device, mesh=mesh, in_specs=in_specs, out_specs=out_specs, check_vma=False)
```

```python
import jax
import jax.numpy as jnp
from jax import lax
from jax.experimental import pallas as pl
from jax.experimental.pallas import tpu as pltpu
from jax.sharding import PartitionSpec as P


def gelu_parts(pre):
    cdf = 0.5 * (1.0 + lax.erf(pre * 0.7071067811865476))
    slope = cdf + pre * jnp.exp(-0.5 * pre * pre) * 0.3989422804014327
    return (pre * cdf, slope)


def softmax_along(values, axis):
    top = jnp.max(values, axis=axis, keepdims=True)
    expo = jnp.exp(values - top)
    return expo / jnp.sum(expo, axis=axis, keepdims=True)


def dot(a, b, contract):
    return lax.dot_general(a, b, (contract, ((), ())), preferred_element_type=jnp.float32)


def in_hbm(value):
    return pltpu.with_memory_space_constraint(value, pltpu.HBM)


NN, NT, TN = ((1,), (0,)), ((1,), (1,)), ((0,), (0,))


def chunk_count(size, wanted):
    while size % wanted or (size // wanted) % 256 and wanted > 1:
        wanted -= 1
    return wanted


CHUNKS, AHEAD, FLIGHT = 8, 3, 8


def first_columns(hid):
    chunks = chunk_count(hid, CHUNKS)
    return min(AHEAD, chunks) * (hid // chunks)


def row_kind(shape, mine):
    return (lax.broadcasted_iota(jnp.int32, shape, 0) // mine) % 2


def slot_rows(slots, mine, wide, kind=None):
    shape = (2 * slots, slots) if wide else (slots, 2 * slots)
    row = lax.broadcasted_iota(jnp.int32, shape, 0 if wide else 1)
    slot = lax.broadcasted_iota(jnp.int32, shape, 1 if wide else 0)
    hit = (row // (2 * mine)) * mine + row % mine == slot
    if kind is not None:
        hit = hit & ((row // mine) % 2 == kind)
    return jnp.where(hit, 1.0, 0.0).astype(jnp.bfloat16)


def route_kernel(
    mine, tok_hbm, out_hbm, par_hbm, win_hbm, wout_hbm,
    sent_ref, mix_ref, win_v, wout_v, tok_v, out_v, par_v, sems,
):
    slots, first = par_v.shape[0], win_v.shape[1]
    loads = [
        pltpu.make_async_copy(par_hbm, par_v, sems.at[0]),
        pltpu.make_async_copy(tok_hbm, tok_v, sems.at[1]),
        pltpu.make_async_copy(out_hbm, out_v, sems.at[2]),
        pltpu.make_async_copy(win_hbm.at[0, :, pl.ds(0, first)], win_v, sems.at[3]),
        pltpu.make_async_copy(wout_hbm.at[0, pl.ds(0, first), :], wout_v, sems.at[4]),
    ]
    for load in loads:
        load.start()
    loads[0].wait()
    par = dot(slot_rows(slots, mine, True), par_v[...], NN).astype(jnp.bfloat16)
    loads[1].wait()
    for image in range(tok_v.shape[0]):
        tok = tok_v[image]
        logits = dot(par, tok, NT)
        dispatch = softmax_along(logits, 1)
        expo = jnp.exp(logits - jnp.max(logits, axis=0, keepdims=True))
        combine = expo / (0.5 * jnp.sum(expo, axis=0, keepdims=True))
        is_in = row_kind(logits.shape, mine) == 0
        mix_ref[image] = jnp.where(is_in, dispatch, combine)
        left = jnp.where(is_in, dispatch, 0.0).astype(jnp.bfloat16)
        right = jnp.where(is_in, 0.0, combine).astype(jnp.bfloat16)
        both = dot(left, tok, NN)
        if image == 0:
            loads[2].wait()
        both = both + dot(right, out_v[image], NN)
        for k in range(slots // mine):
            sent_ref[k, image] = both[2 * mine * k : 2 * mine * (k + 1)].astype(jnp.bfloat16)
    loads[3].wait()
    loads[4].wait()


def route_forward(tokens, grad_out, param_t, weight_in, weight_out, owners):
    images, patches, width = tokens.shape
    slots = param_t.shape[0]
    mine = slots // owners
    first = first_columns(weight_in.shape[2])
    vmem = pl.BlockSpec(memory_space=pltpu.VMEM)
    hbm = pl.BlockSpec(memory_space=pl.ANY)
    return pl.pallas_call(
        lambda *refs: route_kernel(mine, *refs),
        in_specs=[hbm] * 5,
        out_specs=[vmem] * 4,
        out_shape=[
            jax.ShapeDtypeStruct((owners, images, 2 * mine, width), jnp.bfloat16),
            jax.ShapeDtypeStruct((images, 2 * slots, patches), jnp.float32),
            jax.ShapeDtypeStruct((width, first), jnp.bfloat16),
            jax.ShapeDtypeStruct((first, width), jnp.bfloat16),
        ],
        scratch_shapes=[
            pltpu.VMEM(tokens.shape, jnp.bfloat16),
            pltpu.VMEM(grad_out.shape, jnp.bfloat16),
            pltpu.VMEM(param_t.shape, jnp.bfloat16),
            pltpu.SemaphoreType.DMA((5,)),
        ],
        compiler_params=pltpu.CompilerParams(vmem_limit_bytes=16 << 20),
        name="route_forward",
    )(in_hbm(tokens), in_hbm(grad_out), in_hbm(param_t), in_hbm(weight_in), in_hbm(weight_out))


def route_back_kernel(mine, side_ref, back_ref, mix_ref, tok_ref, out_ref, rows_ref, dl_ref, keep_ref, give_ref, raw, part):
    slots = dl_ref.shape[1]
    total = None
    for image in range(tok_ref.shape[0]):
        for k in range(slots // mine):
            raw[2 * mine * k : 2 * mine * (k + 1), :] = back_ref[k, image].astype(jnp.float32)
        rows = raw[...].astype(jnp.bfloat16)
        rows_ref[image] = rows
        tok = tok_ref[image]
        mix = mix_ref[image]
        is_in = row_kind(mix.shape, mine) == 0
        d = jnp.where(is_in, dot(rows, tok, NT), dot(rows, out_ref[image], NT))
        weighed = mix * d
        over_patches = jnp.sum(weighed, axis=1, keepdims=True)
        over_slots = jnp.sum(jnp.where(is_in, 0.0, weighed), axis=0, keepdims=True)
        term = mix * (d - jnp.where(is_in, over_patches, over_slots))
        pair = (term + pltpu.roll(term, 2 * slots - mine, 0)).astype(jnp.bfloat16)
        dl = dot(slot_rows(slots, mine, False, 0), pair, NN).astype(jnp.bfloat16)
        dl_ref[image] = dl
        local = dot(dl, tok, NN)
        total = local if total is None else total + local
    half = slots // 2
    part[...] = total
    side = side_ref[0]
    keep_ref[...] = part[pl.ds(pl.multiple_of(side * half, half), half), :].astype(jnp.bfloat16)
    give_ref[...] = part[pl.ds(pl.multiple_of((1 - side) * half, half), half), :].astype(jnp.bfloat16)


def route_back(side, back, mix, tokens, grad_out):
    owners, images, block, width = back.shape
    mine = block // 2
    slots = owners * mine
    vmem = pl.BlockSpec(memory_space=pltpu.VMEM)
    return pl.pallas_call(
        lambda *refs: route_back_kernel(mine, *refs),
        in_specs=[pl.BlockSpec(memory_space=pltpu.SMEM)] + [vmem] * 4,
        out_specs=[vmem] * 4,
        out_shape=[
            jax.ShapeDtypeStruct((images, 2 * slots, width), jnp.bfloat16),
            jax.ShapeDtypeStruct((images, slots, tokens.shape[1]), jnp.bfloat16),
            jax.ShapeDtypeStruct((slots // 2, width), jnp.bfloat16),
            jax.ShapeDtypeStruct((slots // 2, width), jnp.bfloat16),
        ],
        scratch_shapes=[
            pltpu.VMEM((2 * slots, width), jnp.float32),
            pltpu.VMEM((slots, width), jnp.float32),
        ],
        compiler_params=pltpu.CompilerParams(vmem_limit_bytes=16 << 20),
        name="route_back",
    )(side, back, mix, tokens, grad_out)


def token_grad_kernel(mine, mix_ref, rows_ref, dl_ref, par_ref, grad_ref):
    mix = mix_ref[0]
    left = jnp.where(row_kind(mix.shape, mine) == 0, mix, 0.0).astype(jnp.bfloat16)
    grad_ref[0] = (dot(left, rows_ref[0], TN) + dot(dl_ref[0], par_ref[...], TN)).astype(jnp.bfloat16)


def token_grads(mine, mix, rows, dl, param_t):
    images, twice, patches = mix.shape
    slots, width = param_t.shape
    return pl.pallas_call(
        lambda *refs: token_grad_kernel(mine, *refs),
        grid=(images,),
        in_specs=[
            pl.BlockSpec((1, twice, patches), lambda i: (i, 0, 0)),
            pl.BlockSpec((1, twice, width), lambda i: (i, 0, 0)),
            pl.BlockSpec((1, slots, patches), lambda i: (i, 0, 0)),
            pl.BlockSpec((slots, width), lambda i: (0, 0)),
        ],
        out_specs=pl.BlockSpec((1, patches, width), lambda i: (i, 0, 0)),
        out_shape=jax.ShapeDtypeStruct((images, patches, width), jnp.bfloat16),
        compiler_params=pltpu.CompilerParams(vmem_limit_bytes=16 << 20),
        name="token_grads",
    )(mix, rows, dl, param_t)


def expert_body(
    experts, chunks, x_ref, first_in, first_out, win_hbm, wout_hbm,
    part_ref, give_ref, hid_ref, dpre_ref, win_v, wout_v, win_t, wout_t, sems,
):
    own = part_ref.shape[1]
    step = win_v.shape[2] // chunks
    order = [(e, c) for e in range(experts) for c in range(chunks)]
    held = first_in.shape[1] // step

    def copies(k):
        e, c = order[k]
        cols = pl.ds(c * step, step)
        return (
            pltpu.make_async_copy(win_hbm.at[e, :, cols], win_v.at[e, :, cols], sems.at[0, e, c]),
            pltpu.make_async_copy(wout_hbm.at[e, cols, :], wout_v.at[e, cols, :], sems.at[1, e, c]),
        )

    def start(k):
        if k < len(order):
            for copy in copies(k):
                copy.start()

    def weights(k):
        e, c = order[k]
        cols = pl.ds(c * step, step)
        if k < held:
            return first_in.at[:, cols], first_out.at[cols, :]
        return win_v.at[e, :, cols], wout_v.at[e, cols, :]

    groups = {held: 1}
    k = held + 1
    while k < len(order):
        groups[k] = min(2, len(order) - k)
        k += groups[k]

    for k in range(held, held + FLIGHT):
        start(k)
    ready = out = grad = None
    for k in range(len(order) + 1):
        for arriving in range(k, k + groups.get(k, 0)):
            if arriving < len(order):
                for copy in copies(arriving):
                    copy.wait()
                start(arriving + FLIGHT)
        before = ready
        if k < len(order):
            w1, w2 = weights(k)
            e = order[k][0]
            win_t[k] = w1[...].T
            wout_t[k] = w2[...].T
            ready = dot(x_ref[e], w1[...], NN), dot(x_ref[experts + e], wout_t[k], NN)
        if before is None:
            continue
        e, c = order[k - 1]
        w2 = weights(k - 1)[1]
        cols = pl.ds(c * step, step)
        pre, back = before
        value, slope = gelu_parts(pre)
        hidden = value.astype(jnp.bfloat16)
        dpre = (back * slope).astype(jnp.bfloat16)
        hid_ref[e, :, cols] = hidden
        dpre_ref[e, :, cols] = dpre
        o = dot(hidden, w2[...], NN)
        d = dot(dpre, win_t[k - 1], NN)
        out, grad = (o, d) if c == 0 else (out + o, grad + d)
        if c == chunks - 1:
            part_ref[e] = grad[:own]
            part_ref[experts + e] = out[:own]
            if own < out.shape[0]:
                give_ref[e] = grad[own:].astype(jnp.bfloat16)
                give_ref[experts + e] = out[own:].astype(jnp.bfloat16)
            else:
                give_ref[...] = jnp.zeros_like(give_ref)


def expert_forward(rows_in, first_in, first_out, weight_in, weight_out, own):
    experts, width, hid = weight_in.shape
    rows = rows_in.shape[1]
    chunks = chunk_count(hid, CHUNKS)
    vmem = pl.BlockSpec(memory_space=pltpu.VMEM)
    hbm = pl.BlockSpec(memory_space=pl.ANY)
    return pl.pallas_call(
        lambda *refs: expert_body(experts, chunks, *refs),
        in_specs=[vmem, vmem, vmem, hbm, hbm],
        out_specs=[vmem, vmem, vmem, vmem],
        out_shape=[
            jax.ShapeDtypeStruct((2 * experts, own, width), jnp.float32),
            jax.ShapeDtypeStruct((2 * experts, max(rows - own, 8), width), jnp.bfloat16),
            jax.ShapeDtypeStruct((experts, rows, hid), jnp.bfloat16),
            jax.ShapeDtypeStruct((experts, rows, hid), jnp.bfloat16),
        ],
        scratch_shapes=[
            pltpu.VMEM((experts, width, hid), jnp.bfloat16),
            pltpu.VMEM((experts, hid, width), jnp.bfloat16),
            pltpu.VMEM((experts * chunks, hid // chunks, width), jnp.bfloat16),
            pltpu.VMEM((experts * chunks, width, hid // chunks), jnp.bfloat16),
            pltpu.SemaphoreType.DMA((2, experts, chunks)),
        ],
        compiler_params=pltpu.CompilerParams(vmem_limit_bytes=40 << 20),
        name="expert_forward",
    )(rows_in, first_in, first_out, in_hbm(weight_in), in_hbm(weight_out))


def weight_grad_kernel(x_ref, g_ref, hid_ref, dpre_ref, gin_ref, gout_ref):
    gin_ref[0] = dot(x_ref[0], dpre_ref[0], TN).astype(jnp.bfloat16)
    gout_ref[0] = dot(hid_ref[0], g_ref[0], TN).astype(jnp.bfloat16)


def weight_grads(rows_in, hidden, dpre):
    experts, rows, hid = hidden.shape
    width = rows_in.shape[2]
    chunks = chunk_count(hid, 4)
    step = hid // chunks
    return pl.pallas_call(
        weight_grad_kernel,
        grid=(experts, chunks),
        in_specs=[
            pl.BlockSpec((1, rows, width), lambda e, c: (e, 0, 0)),
            pl.BlockSpec((1, rows, width), lambda e, c: (experts + e, 0, 0)),
            pl.BlockSpec((1, rows, step), lambda e, c: (e, 0, c)),
            pl.BlockSpec((1, rows, step), lambda e, c: (e, 0, c)),
        ],
        out_specs=[
            pl.BlockSpec((1, width, step), lambda e, c: (e, 0, c)),
            pl.BlockSpec((1, step, width), lambda e, c: (e, c, 0)),
        ],
        out_shape=[
            jax.ShapeDtypeStruct((experts, width, hid), jnp.bfloat16),
            jax.ShapeDtypeStruct((experts, hid, width), jnp.bfloat16),
        ],
        compiler_params=pltpu.CompilerParams(vmem_limit_bytes=24 << 20),
        name="weight_grads",
    )(rows_in, rows_in, hidden, dpre)


def swap(value, axis, mask):
    size = lax.axis_size(axis)
    return lax.ppermute(value, axis, [(k, k ^ mask) for k in range(size)])


def is_pow2(n):
    return n & (n - 1) == 0


def sum_bits(acc, axis, first_bit):
    size = lax.axis_size(axis)
    bit = first_bit
    while bit < size:
        sent = acc.astype(jnp.bfloat16)
        own = sent.astype(jnp.float32)
        if 2 * bit < size:
            a, b, c = (swap(sent, axis, m).astype(jnp.float32) for m in (bit, 2 * bit, 3 * bit))
            acc = (own + a) + (b + c)
            bit *= 4
        else:
            acc = own + swap(sent, axis, bit).astype(jnp.float32)
            bit *= 2
    return acc


def sum_everywhere(keep, give, side):
    ex, ey = lax.axis_size("ex"), lax.axis_size("ey")
    if not (is_pow2(ex) and is_pow2(ey)):
        low = jnp.where(side == 0, keep, give).astype(jnp.float32)
        high = jnp.where(side == 0, give, keep).astype(jnp.float32)
        return lax.psum(jnp.concatenate((low, high), axis=0), ("ex", "ey"))
    acc = keep.astype(jnp.float32) + swap(give, "ex", 1).astype(jnp.float32)
    acc = sum_bits(acc, "ex", 2)
    acc = sum_bits(acc, "ey", 1)
    sent = acc.astype(jnp.bfloat16)
    own = sent.astype(jnp.float32)
    other = swap(sent, "ex", 1)
    other = other.astype(jnp.float32)
    return jnp.concatenate((jnp.where(side == 0, own, other), jnp.where(side == 0, other, own)), axis=0)


def gather_ex(value):
    if lax.axis_size("ex") == 2:
        return jnp.stack((value, swap(value, "ex", 1)))
    return lax.all_gather(value, "ex", axis=0)


def join_kernel(keep_ref, got_ref, sum_hbm, sum_v, sem):
    block, rows, width = keep_ref.shape
    total = (keep_ref[...] + got_ref[...].astype(jnp.float32)).reshape(block * rows, width)
    shape = (block * rows, block * rows)
    to = lax.broadcasted_iota(jnp.int32, shape, 0)
    at = lax.broadcasted_iota(jnp.int32, shape, 1)
    move = jnp.where((to % block) * rows + to // block == at, 1.0, 0.0).astype(jnp.bfloat16)
    moved = dot(move, total.astype(jnp.bfloat16), NN)
    for k in range(rows):
        sum_v[k] = moved[block * k : block * (k + 1)].astype(jnp.bfloat16)
    copy = pltpu.make_async_copy(sum_v, sum_hbm, sem)
    copy.start()
    copy.wait()


def join(keep, got):
    block, rows, width = keep.shape
    vmem = pl.BlockSpec(memory_space=pltpu.VMEM)
    return pl.pallas_call(
        lambda *refs: join_kernel(*refs),
        in_specs=[vmem, vmem],
        out_specs=pl.BlockSpec(memory_space=pl.ANY),
        out_shape=pltpu.HBM((rows, block, width), jnp.bfloat16),
        scratch_shapes=[pltpu.VMEM((rows, block, width), jnp.bfloat16), pltpu.SemaphoreType.DMA],
        compiler_params=pltpu.CompilerParams(vmem_limit_bytes=16 << 20),
        name="join",
    )(keep, got)


def per_device(tokens, slot_param, weight_in, weight_out, grad_out):
    ex, ey = lax.axis_size("ex"), lax.axis_size("ey")
    images, _, width = tokens.shape
    slots = slot_param.shape[1]
    mine = slots // ey
    param_t = slot_param.T
    sent, mix, first_in, first_out = route_forward(tokens, grad_out, param_t, weight_in, weight_out, ey)
    moved = lax.all_to_all(sent.reshape(ey * images, 2 * mine, width), "ey", split_axis=0, concat_axis=0, tiled=True)
    arrived = gather_ex(moved)
    rows = ex * ey * images
    rows_in = arrived.reshape(rows, 2 * mine, width).transpose(1, 0, 2)
    own = rows // 2 if ex == 2 else rows
    keep_rows, give_rows, hidden, dpre = expert_forward(
        rows_in, first_in, first_out, weight_in, weight_out, own
    )
    if ex == 2:
        summed = join(keep_rows, swap(give_rows, "ex", 1))
    else:
        blocks = keep_rows.astype(jnp.bfloat16).transpose(1, 0, 2).reshape(ex, ey * images, 2 * mine, width)
        summed = lax.psum_scatter(blocks, "ex", scatter_dimension=0)
    back = lax.all_to_all(summed, "ey", split_axis=0, concat_axis=0, tiled=True)
    grad_win, grad_wout = weight_grads(rows_in, hidden, dpre)
    side = lax.axis_index("ex") % 2
    back_rows, logit_grad, keep, give = route_back(
        side.reshape(1), back.reshape(ey, images, 2 * mine, width), mix, tokens, grad_out
    )
    grad_param = sum_everywhere(keep, give, side).T
    grad_tokens = token_grads(mine, mix, back_rows, logit_grad, param_t)
    return (grad_tokens, grad_param, grad_win, grad_wout)


def solution(mesh):
    in_specs = (
        P(("ex", "ey"), None, None),
        P(),
        P("ey", None, "ex"),
        P("ey", "ex", None),
        P(("ex", "ey"), None, None),
    )
    out_specs = (P(("ex", "ey"), None, None), P(), P("ey", None, "ex"), P("ey", "ex", None))

    return jax.shard_map(per_device, mesh=mesh, in_specs=in_specs, out_specs=out_specs, check_vma=False)
```

```python
import jax
import jax.numpy as jnp
from jax import lax
from jax.experimental import pallas as pl
from jax.experimental.pallas import tpu as pltpu
from jax.sharding import PartitionSpec as P


def gelu_parts(pre):
    cdf = 0.5 * (1.0 + lax.erf(pre * 0.7071067811865476))
    slope = cdf + pre * jnp.exp(-0.5 * pre * pre) * 0.3989422804014327
    return (pre * cdf, slope)


def softmax_along(values, axis):
    top = jnp.max(values, axis=axis, keepdims=True)
    expo = jnp.exp(values - top)
    return expo / jnp.sum(expo, axis=axis, keepdims=True)


def dot(a, b, contract):
    return lax.dot_general(a, b, (contract, ((), ())), preferred_element_type=jnp.float32)


def in_hbm(value):
    return pltpu.with_memory_space_constraint(value, pltpu.HBM)


NN, NT, TN = ((1,), (0,)), ((1,), (1,)), ((0,), (0,))


def chunk_count(size, wanted):
    while size % wanted or (size // wanted) % 256 and wanted > 1:
        wanted -= 1
    return wanted


CHUNKS, AHEAD, FLIGHT = 8, 2, 8


def first_columns(hid):
    chunks = chunk_count(hid, CHUNKS)
    return min(AHEAD, chunks) * (hid // chunks)


def route_kernel(
    mine, tok_hbm, out_hbm, par_hbm, sent_ref, disp_ref, comb_ref, tok_v, out_v, par_v, sems
):
    slots = par_v.shape[0]
    loads = [
        pltpu.make_async_copy(par_hbm, par_v, sems.at[0]),
        pltpu.make_async_copy(tok_hbm, tok_v, sems.at[1]),
        pltpu.make_async_copy(out_hbm, out_v, sems.at[2]),
    ]
    for load in loads:
        load.start()
    loads[0].wait()
    loads[1].wait()
    for image in range(tok_v.shape[0]):
        tok = tok_v[image]
        logits = dot(par_v[...], tok, NT)
        dispatch = softmax_along(logits, 1)
        combine = softmax_along(logits, 0)
        disp_ref[image] = dispatch
        comb_ref[image] = combine
        slot_in = dot(dispatch.astype(jnp.bfloat16), tok, NN)
        if image == 0:
            loads[2].wait()
        slot_cot = dot(combine.astype(jnp.bfloat16), out_v[image], NN)
        for kind, values in enumerate((slot_in, slot_cot)):
            for k in range(slots // mine):
                sent_ref[kind * (slots // mine) + k, image] = values[mine * k : mine * (k + 1)].astype(jnp.bfloat16)


def route_forward(tokens, grad_out, param_t, owners):
    images, patches, width = tokens.shape
    slots = param_t.shape[0]
    mine = slots // owners
    vmem = pl.BlockSpec(memory_space=pltpu.VMEM)
    hbm = pl.BlockSpec(memory_space=pl.ANY)
    return pl.pallas_call(
        lambda *refs: route_kernel(mine, *refs),
        in_specs=[hbm] * 3,
        out_specs=[vmem] * 3,
        out_shape=[
            jax.ShapeDtypeStruct((2 * owners, images, mine, width), jnp.bfloat16),
            jax.ShapeDtypeStruct((images, slots, patches), jnp.float32),
            jax.ShapeDtypeStruct((images, slots, patches), jnp.float32),
        ],
        scratch_shapes=[
            pltpu.VMEM(tokens.shape, jnp.bfloat16),
            pltpu.VMEM(grad_out.shape, jnp.bfloat16),
            pltpu.VMEM(param_t.shape, jnp.bfloat16),
            pltpu.SemaphoreType.DMA((3,)),
        ],
        compiler_params=pltpu.CompilerParams(vmem_limit_bytes=16 << 20),
        name="route_forward",
    )(in_hbm(tokens), in_hbm(grad_out), in_hbm(param_t))


def fetch_kernel(win_hbm, wout_hbm, win_v, wout_v, sems):
    first = win_v.shape[1]
    loads = (
        pltpu.make_async_copy(win_hbm.at[0, :, pl.ds(0, first)], win_v, sems.at[0]),
        pltpu.make_async_copy(wout_hbm.at[0, pl.ds(0, first), :], wout_v, sems.at[1]),
    )
    for load in loads:
        load.start()
    for load in loads:
        load.wait()


def fetch_first(weight_in, weight_out):
    width = weight_in.shape[1]
    first = first_columns(weight_in.shape[2])
    return pl.pallas_call(
        fetch_kernel,
        in_specs=[pl.BlockSpec(memory_space=pl.ANY)] * 2,
        out_specs=[pl.BlockSpec(memory_space=pltpu.VMEM)] * 2,
        out_shape=[
            jax.ShapeDtypeStruct((width, first), jnp.bfloat16),
            jax.ShapeDtypeStruct((first, width), jnp.bfloat16),
        ],
        scratch_shapes=[pltpu.SemaphoreType.DMA((2,))],
        compiler_params=pltpu.CompilerParams(vmem_limit_bytes=8 << 20),
        name="fetch_first",
    )(in_hbm(weight_in), in_hbm(weight_out))


def route_back_kernel(
    side_ref, back_ref, disp_ref, comb_ref, tok_ref, out_ref, grad_ref, dl_ref, keep_ref, give_ref, raw, part
):
    blocks, _, mine, _ = back_ref.shape
    slots = blocks // 2 * mine
    total = None
    for image in range(tok_ref.shape[0]):
        for k in range(blocks):
            raw[mine * k : mine * (k + 1), :] = back_ref[k, image].astype(jnp.float32)
        grad_slot = raw[:slots, :].astype(jnp.bfloat16)
        slot_out = raw[slots:, :].astype(jnp.bfloat16)
        grad_ref[image] = grad_slot
        tok = tok_ref[image]
        dispatch = disp_ref[image]
        combine = comb_ref[image]
        d_dispatch = dot(grad_slot, tok, NT)
        d_combine = dot(slot_out, out_ref[image], NT)
        d_logits = dispatch * (d_dispatch - jnp.sum(dispatch * d_dispatch, axis=1, keepdims=True))
        d_logits = d_logits + combine * (d_combine - jnp.sum(combine * d_combine, axis=0, keepdims=True))
        dl = d_logits.astype(jnp.bfloat16)
        dl_ref[image] = dl
        local = dot(dl, tok, NN)
        total = local if total is None else total + local
    half = slots // 2
    part[...] = total
    side = side_ref[0]
    keep_ref[...] = part[pl.ds(pl.multiple_of(side * half, half), half), :].astype(jnp.bfloat16)
    give_ref[...] = part[pl.ds(pl.multiple_of((1 - side) * half, half), half), :].astype(jnp.bfloat16)


def route_back(side, back, dispatch, combine, tokens, grad_out):
    blocks, images, mine, width = back.shape
    slots = blocks // 2 * mine
    vmem = pl.BlockSpec(memory_space=pltpu.VMEM)
    return pl.pallas_call(
        route_back_kernel,
        in_specs=[pl.BlockSpec(memory_space=pltpu.SMEM)] + [vmem] * 5,
        out_specs=[vmem] * 4,
        out_shape=[
            jax.ShapeDtypeStruct((images, slots, width), jnp.bfloat16),
            jax.ShapeDtypeStruct((images, slots, tokens.shape[1]), jnp.bfloat16),
            jax.ShapeDtypeStruct((slots // 2, width), jnp.bfloat16),
            jax.ShapeDtypeStruct((slots // 2, width), jnp.bfloat16),
        ],
        scratch_shapes=[
            pltpu.VMEM((2 * slots, width), jnp.float32),
            pltpu.VMEM((slots, width), jnp.float32),
        ],
        compiler_params=pltpu.CompilerParams(vmem_limit_bytes=16 << 20),
        name="route_back",
    )(side, back, dispatch, combine, tokens, grad_out)


def token_grad_kernel(disp_ref, slot_ref, dl_ref, par_ref, grad_ref):
    left = jnp.concatenate((disp_ref[0].astype(jnp.bfloat16), dl_ref[0]), axis=0)
    right = jnp.concatenate((slot_ref[0], par_ref[...]), axis=0)
    grad_ref[0] = dot(left, right, TN).astype(jnp.bfloat16)


def token_grads(dispatch, grad_slot, dl, param_t):
    images, slots, patches = dispatch.shape
    width = param_t.shape[1]
    table = pl.BlockSpec((1, slots, patches), lambda i: (i, 0, 0))
    return pl.pallas_call(
        token_grad_kernel,
        grid=(images,),
        in_specs=[
            table,
            pl.BlockSpec((1, slots, width), lambda i: (i, 0, 0)),
            table,
            pl.BlockSpec((slots, width), lambda i: (0, 0)),
        ],
        out_specs=pl.BlockSpec((1, patches, width), lambda i: (i, 0, 0)),
        out_shape=jax.ShapeDtypeStruct((images, patches, width), jnp.bfloat16),
        compiler_params=pltpu.CompilerParams(vmem_limit_bytes=16 << 20),
        name="token_grads",
    )(dispatch, grad_slot, dl, param_t)


def expert_body(
    experts, chunks, place_ref, x_ref, first_in, first_out, win_hbm, wout_hbm,
    keep_ref, give_ref, hid_ref, dpre_ref, win_v, wout_v, win_t, wout_t, sems,
):
    place = place_ref[0]
    step = win_v.shape[2] // chunks
    order = [(e, c) for e in range(experts) for c in range(chunks)]
    held = first_in.shape[1] // step

    def copies(k):
        e, c = order[k]
        cols = pl.ds(c * step, step)
        return (
            pltpu.make_async_copy(win_hbm.at[e, :, cols], win_v.at[e, :, cols], sems.at[0, e, c]),
            pltpu.make_async_copy(wout_hbm.at[e, cols, :], wout_v.at[e, cols, :], sems.at[1, e, c]),
        )

    def start(k):
        if k < len(order):
            for copy in copies(k):
                copy.start()

    def weights(k):
        e, c = order[k]
        cols = pl.ds(c * step, step)
        if k < held:
            return first_in.at[:, cols], first_out.at[cols, :]
        return win_v.at[e, :, cols], wout_v.at[e, cols, :]

    groups = {held: 1}
    k = held + 1
    while k < len(order):
        groups[k] = min(2, len(order) - k)
        k += groups[k]

    for k in range(held, held + FLIGHT):
        start(k)
    ready = out = grad = None
    for k in range(len(order) + 1):
        for arriving in range(k, k + groups.get(k, 0)):
            if arriving < len(order):
                for copy in copies(arriving):
                    copy.wait()
                start(arriving + FLIGHT)
        before = ready
        if k < len(order):
            w1, w2 = weights(k)
            e = order[k][0]
            win_t[k] = w1[...].T
            wout_t[k] = w2[...].T
            x = x_ref[place * experts + e]
            g = x_ref[(1 - place) * experts + e]
            ready = dot(x, w1[...], NN), dot(g, wout_t[k], NN)
        if before is None:
            continue
        e, c = order[k - 1]
        w2 = weights(k - 1)[1]
        cols = pl.ds(c * step, step)
        pre, back = before
        value, slope = gelu_parts(pre)
        hidden = value.astype(jnp.bfloat16)
        dpre = (back * slope).astype(jnp.bfloat16)
        hid_ref[e, :, cols] = hidden
        dpre_ref[e, :, cols] = dpre
        o = dot(hidden, w2[...], NN)
        d = dot(dpre, win_t[k - 1], NN)
        out, grad = (o, d) if c == 0 else (out + o, grad + d)
        if c == chunks - 1:
            if keep_ref.shape[0] == experts:
                first = place == 0
                keep_ref[e] = jnp.where(first, grad, out)
                give_ref[e] = jnp.where(first, out, grad).astype(jnp.bfloat16)
            else:
                keep_ref[e] = grad
                keep_ref[experts + e] = out
                give_ref[e] = grad.astype(jnp.bfloat16)


def expert_forward(place, rows_in, first_in, first_out, weight_in, weight_out, split):
    experts, width, hid = weight_in.shape
    rows = rows_in.shape[1]
    chunks = chunk_count(hid, CHUNKS)
    vmem = pl.BlockSpec(memory_space=pltpu.VMEM)
    hbm = pl.BlockSpec(memory_space=pl.ANY)
    return pl.pallas_call(
        lambda *refs: expert_body(experts, chunks, *refs),
        in_specs=[pl.BlockSpec(memory_space=pltpu.SMEM), vmem, vmem, vmem, hbm, hbm],
        out_specs=[vmem, vmem, vmem, vmem],
        out_shape=[
            jax.ShapeDtypeStruct((experts if split else 2 * experts, rows, width), jnp.float32),
            jax.ShapeDtypeStruct((experts, rows, width), jnp.bfloat16),
            jax.ShapeDtypeStruct((experts, rows, hid), jnp.bfloat16),
            jax.ShapeDtypeStruct((experts, rows, hid), jnp.bfloat16),
        ],
        scratch_shapes=[
            pltpu.VMEM((experts, width, hid), jnp.bfloat16),
            pltpu.VMEM((experts, hid, width), jnp.bfloat16),
            pltpu.VMEM((experts * chunks, hid // chunks, width), jnp.bfloat16),
            pltpu.VMEM((experts * chunks, width, hid // chunks), jnp.bfloat16),
            pltpu.SemaphoreType.DMA((2, experts, chunks)),
        ],
        compiler_params=pltpu.CompilerParams(vmem_limit_bytes=40 << 20),
        name="expert_forward",
    )(place, rows_in, first_in, first_out, in_hbm(weight_in), in_hbm(weight_out))


def weight_grad_kernel(experts, place_ref, rows_ref, hid_ref, dpre_ref, gin_ref, gout_ref):
    e = pl.program_id(0)
    x = rows_ref[place_ref[0] * experts + e]
    g = rows_ref[(1 - place_ref[0]) * experts + e]
    gin_ref[0] = dot(x, dpre_ref[0], TN).astype(jnp.bfloat16)
    gout_ref[0] = dot(hid_ref[0], g, TN).astype(jnp.bfloat16)


def weight_grads(place, rows_in, hidden, dpre):
    experts, rows, hid = hidden.shape
    width = rows_in.shape[2]
    chunks = chunk_count(hid, 4)
    step = hid // chunks
    return pl.pallas_call(
        lambda *refs: weight_grad_kernel(experts, *refs),
        grid=(experts, chunks),
        in_specs=[
            pl.BlockSpec(memory_space=pltpu.SMEM),
            pl.BlockSpec((2 * experts, rows, width), lambda e, c: (0, 0, 0)),
            pl.BlockSpec((1, rows, step), lambda e, c: (e, 0, c)),
            pl.BlockSpec((1, rows, step), lambda e, c: (e, 0, c)),
        ],
        out_specs=[
            pl.BlockSpec((1, width, step), lambda e, c: (e, 0, c)),
            pl.BlockSpec((1, step, width), lambda e, c: (e, c, 0)),
        ],
        out_shape=[
            jax.ShapeDtypeStruct((experts, width, hid), jnp.bfloat16),
            jax.ShapeDtypeStruct((experts, hid, width), jnp.bfloat16),
        ],
        compiler_params=pltpu.CompilerParams(vmem_limit_bytes=24 << 20),
        name="weight_grads",
    )(place, rows_in, hidden, dpre)


def swap(value, axis, mask):
    size = lax.axis_size(axis)
    return lax.ppermute(value, axis, [(k, k ^ mask) for k in range(size)])


def is_pow2(n):
    return n & (n - 1) == 0


def sum_bits(acc, axis, first_bit):
    size = lax.axis_size(axis)
    bit = first_bit
    while bit < size:
        sent = acc.astype(jnp.bfloat16)
        own = sent.astype(jnp.float32)
        if 2 * bit < size:
            got = []
            for mask in (bit, 2 * bit, 3 * bit):
                got.append(swap(sent, axis, mask).astype(jnp.float32))
            a, b, c = got
            acc = (own + a) + (b + c)
            bit *= 4
        else:
            acc = own + swap(sent, axis, bit).astype(jnp.float32)
            bit *= 2
    return acc


def sum_everywhere(keep, give, side):
    ex, ey = lax.axis_size("ex"), lax.axis_size("ey")
    if not (is_pow2(ex) and is_pow2(ey)):
        low = jnp.where(side == 0, keep, give).astype(jnp.float32)
        high = jnp.where(side == 0, give, keep).astype(jnp.float32)
        return lax.psum(jnp.concatenate((low, high), axis=0), ("ex", "ey"))
    acc = keep.astype(jnp.float32) + swap(give, "ex", 1).astype(jnp.float32)
    acc = sum_bits(acc, "ex", 2)
    acc = sum_bits(acc, "ey", 1)
    sent = acc.astype(jnp.bfloat16)
    own = sent.astype(jnp.float32)
    other = swap(sent, "ex", 1)
    other = other.astype(jnp.float32)
    return jnp.concatenate((jnp.where(side == 0, own, other), jnp.where(side == 0, other, own)), axis=0)


def join_kernel(keep_ref, got_ref, sum_hbm, sum_v, sem):
    block, rows, width = keep_ref.shape
    total = (keep_ref[...] + got_ref[...].astype(jnp.float32)).reshape(block * rows, width)
    shape = (block * rows, block * rows)
    to = lax.broadcasted_iota(jnp.int32, shape, 0)
    at = lax.broadcasted_iota(jnp.int32, shape, 1)
    move = jnp.where((to % block) * rows + to // block == at, 1.0, 0.0).astype(jnp.bfloat16)
    moved = dot(move, total.astype(jnp.bfloat16), NN)
    for k in range(rows):
        sum_v[k] = moved[block * k : block * (k + 1)].astype(jnp.bfloat16)
    copy = pltpu.make_async_copy(sum_v, sum_hbm, sem)
    copy.start()
    copy.wait()


def join(keep, got):
    block, rows, width = keep.shape
    vmem = pl.BlockSpec(memory_space=pltpu.VMEM)
    return pl.pallas_call(
        join_kernel,
        in_specs=[vmem, vmem],
        out_specs=pl.BlockSpec(memory_space=pl.ANY),
        out_shape=pltpu.HBM((rows, block, width), jnp.bfloat16),
        scratch_shapes=[pltpu.VMEM((rows, block, width), jnp.bfloat16), pltpu.SemaphoreType.DMA],
        compiler_params=pltpu.CompilerParams(vmem_limit_bytes=16 << 20),
        name="join",
    )(keep, got)


def per_device(tokens, slot_param, weight_in, weight_out, grad_out):
    ex, ey = lax.axis_size("ex"), lax.axis_size("ey")
    images, _, width = tokens.shape
    slots = slot_param.shape[1]
    mine = slots // ey
    param_t = slot_param.T
    sent, dispatch, combine = route_forward(tokens, grad_out, param_t, ey)
    first_in, first_out = fetch_first(weight_in, weight_out)
    side = lax.axis_index("ex") % 2
    rows = ex * ey * images
    paired = ex == 2
    if paired:
        sent = sent.reshape(2 * ey, images * mine, width)
        own = lax.all_to_all(sent, ("ex", "ey"), split_axis=0, concat_axis=0, tiled=True)
        other = swap(own, "ex", 1)
        place = side.reshape(1)
        kinds = jnp.stack((own, other))
        rows_in = kinds.reshape(2, rows, mine, width).transpose(0, 2, 1, 3).reshape(2 * mine, rows, width)
    else:
        place = jnp.zeros((1,), jnp.int32)
        sent = sent.reshape(2, ey, images, mine, width).transpose(1, 2, 0, 3, 4)
        sent = sent.reshape(ey * images, 2 * mine, width)
        moved = lax.all_to_all(sent, "ey", split_axis=0, concat_axis=0, tiled=True)
        arrived = lax.all_gather(moved, "ex", axis=0)
        rows_in = arrived.reshape(rows, 2 * mine, width).transpose(1, 0, 2)
    keep_rows, give_rows, hidden, dpre = expert_forward(
        place, rows_in, first_in, first_out, weight_in, weight_out, paired
    )
    if paired:
        summed = join(keep_rows, swap(give_rows, "ex", 1)).reshape(2 * ey, images * mine, width)
        back = lax.all_to_all(summed, ("ex", "ey"), split_axis=0, concat_axis=0, tiled=True)
        back = back.reshape(2 * ey, images, mine, width)
    else:
        blocks = keep_rows.astype(jnp.bfloat16).transpose(1, 0, 2).reshape(ex, ey * images, 2 * mine, width)
        summed = lax.psum_scatter(blocks, "ex", scatter_dimension=0)
        back = lax.all_to_all(summed, "ey", split_axis=0, concat_axis=0, tiled=True)
        back = back.reshape(ey, images, 2, mine, width).transpose(2, 0, 1, 3, 4)
        back = back.reshape(2 * ey, images, mine, width)
    grad_win, grad_wout = weight_grads(place, rows_in, hidden, dpre)
    grad_slot, logit_grad, keep, give = route_back(side.reshape(1), back, dispatch, combine, tokens, grad_out)
    grad_param = sum_everywhere(keep, give, side).T
    grad_tokens = token_grads(dispatch, grad_slot, logit_grad, param_t)
    return (grad_tokens, grad_param, grad_win, grad_wout)


def solution(mesh):
    in_specs = (
        P(("ex", "ey"), None, None),
        P(),
        P("ey", None, "ex"),
        P("ey", "ex", None),
        P(("ex", "ey"), None, None),
    )
    out_specs = (P(("ex", "ey"), None, None), P(), P("ey", None, "ex"), P("ey", "ex", None))

    return jax.shard_map(per_device, mesh=mesh, in_specs=in_specs, out_specs=out_specs, check_vma=False)
```

```python
import jax
import jax.numpy as jnp
from jax import lax
from jax.experimental import pallas as pl
from jax.experimental.pallas import tpu as pltpu
from jax.sharding import PartitionSpec as P


def gelu_parts(pre):
    cdf = 0.5 * (1.0 + lax.erf(pre * 0.7071067811865476))
    slope = cdf + pre * jnp.exp(-0.5 * pre * pre) * 0.3989422804014327
    return (pre * cdf, slope)


def softmax_along(values, axis):
    top = jnp.max(values, axis=axis, keepdims=True)
    expo = jnp.exp(values - top)
    return expo / jnp.sum(expo, axis=axis, keepdims=True)


def dot(a, b, contract):
    return lax.dot_general(a, b, (contract, ((), ())), preferred_element_type=jnp.float32)


def in_hbm(value):
    return pltpu.with_memory_space_constraint(value, pltpu.HBM)


NN, NT, TN = ((1,), (0,)), ((1,), (1,)), ((0,), (0,))


def chunk_count(size, wanted):
    while size % wanted or (size // wanted) % 256 and wanted > 1:
        wanted -= 1
    return wanted


CHUNKS, AHEAD, FLIGHT = 8, 2, 8


def first_columns(hid):
    chunks = chunk_count(hid, CHUNKS)
    return min(AHEAD, chunks) * (hid // chunks)


def route_kernel(
    mine, tok_hbm, out_hbm, par_hbm, sent_ref, disp_ref, comb_ref, tok_v, out_v, par_v, sems
):
    slots = par_v.shape[0]
    loads = [
        pltpu.make_async_copy(par_hbm, par_v, sems.at[0]),
        pltpu.make_async_copy(tok_hbm, tok_v, sems.at[1]),
        pltpu.make_async_copy(out_hbm, out_v, sems.at[2]),
    ]
    for load, rank in zip(loads, (0, 0, 1)):
        load.start(priority=rank)
    loads[0].wait()
    loads[1].wait()
    for image in range(tok_v.shape[0]):
        tok = tok_v[image]
        logits = dot(par_v[...], tok, NT)
        dispatch = softmax_along(logits, 1)
        combine = softmax_along(logits, 0)
        disp_ref[image] = dispatch
        comb_ref[image] = combine
        slot_in = dot(dispatch.astype(jnp.bfloat16), tok, NN)
        if image == 0:
            loads[2].wait()
        slot_cot = dot(combine.astype(jnp.bfloat16), out_v[image], NN)
        for kind, values in enumerate((slot_in, slot_cot)):
            for k in range(slots // mine):
                sent_ref[kind * (slots // mine) + k, image] = values[mine * k : mine * (k + 1)].astype(jnp.bfloat16)


def route_forward(tokens, grad_out, param_t, owners):
    images, patches, width = tokens.shape
    slots = param_t.shape[0]
    mine = slots // owners
    vmem = pl.BlockSpec(memory_space=pltpu.VMEM)
    hbm = pl.BlockSpec(memory_space=pl.ANY)
    return pl.pallas_call(
        lambda *refs: route_kernel(mine, *refs),
        in_specs=[hbm] * 3,
        out_specs=[vmem] * 3,
        out_shape=[
            jax.ShapeDtypeStruct((2 * owners, images, mine, width), jnp.bfloat16),
            jax.ShapeDtypeStruct((images, slots, patches), jnp.float32),
            jax.ShapeDtypeStruct((images, slots, patches), jnp.float32),
        ],
        scratch_shapes=[
            pltpu.VMEM(tokens.shape, jnp.bfloat16),
            pltpu.VMEM(grad_out.shape, jnp.bfloat16),
            pltpu.VMEM(param_t.shape, jnp.bfloat16),
            pltpu.SemaphoreType.DMA((3,)),
        ],
        compiler_params=pltpu.CompilerParams(vmem_limit_bytes=16 << 20),
        name="route_forward",
    )(in_hbm(tokens), in_hbm(grad_out), in_hbm(param_t))


def by_kind(place, own, other):
    first = place == 0
    return jnp.where(first, own, other), jnp.where(first, other, own)


def fetch_kernel(win_hbm, wout_hbm, win_v, wout_v, sems):
    first = win_v.shape[1]
    loads = (
        pltpu.make_async_copy(win_hbm.at[0, :, pl.ds(0, first)], win_v, sems.at[0]),
        pltpu.make_async_copy(wout_hbm.at[0, pl.ds(0, first), :], wout_v, sems.at[1]),
    )
    for load in loads:
        load.start()
    for load in loads:
        load.wait()


def fetch_first(weight_in, weight_out):
    width = weight_in.shape[1]
    first = first_columns(weight_in.shape[2])
    return pl.pallas_call(
        fetch_kernel,
        in_specs=[pl.BlockSpec(memory_space=pl.ANY)] * 2,
        out_specs=[pl.BlockSpec(memory_space=pltpu.VMEM)] * 2,
        out_shape=[
            jax.ShapeDtypeStruct((width, first), jnp.bfloat16),
            jax.ShapeDtypeStruct((first, width), jnp.bfloat16),
        ],
        scratch_shapes=[pltpu.SemaphoreType.DMA((2,))],
        compiler_params=pltpu.CompilerParams(vmem_limit_bytes=8 << 20),
        name="fetch_first",
    )(in_hbm(weight_in), in_hbm(weight_out))


def route_back_kernel(
    side_ref, back_ref, disp_ref, comb_ref, tok_ref, out_ref, grad_ref, dl_ref, keep_ref, give_ref, raw, part
):
    blocks, _, mine, _ = back_ref.shape
    slots = blocks // 2 * mine
    total = None
    for image in range(tok_ref.shape[0]):
        for k in range(blocks):
            raw[mine * k : mine * (k + 1), :] = back_ref[k, image].astype(jnp.float32)
        grad_slot = raw[:slots, :].astype(jnp.bfloat16)
        slot_out = raw[slots:, :].astype(jnp.bfloat16)
        grad_ref[image] = grad_slot
        tok = tok_ref[image]
        dispatch = disp_ref[image]
        combine = comb_ref[image]
        d_dispatch = dot(grad_slot, tok, NT)
        d_combine = dot(slot_out, out_ref[image], NT)
        d_logits = dispatch * (d_dispatch - jnp.sum(dispatch * d_dispatch, axis=1, keepdims=True))
        d_logits = d_logits + combine * (d_combine - jnp.sum(combine * d_combine, axis=0, keepdims=True))
        dl = d_logits.astype(jnp.bfloat16)
        dl_ref[image] = dl
        local = dot(dl, tok, NN)
        total = local if total is None else total + local
    half = slots // 2
    part[...] = total
    side = side_ref[0]
    keep_ref[...] = part[pl.ds(pl.multiple_of(side * half, half), half), :].astype(jnp.bfloat16)
    give_ref[...] = part[pl.ds(pl.multiple_of((1 - side) * half, half), half), :].astype(jnp.bfloat16)


def route_back(side, back, dispatch, combine, tokens, grad_out):
    blocks, images, mine, width = back.shape
    slots = blocks // 2 * mine
    vmem = pl.BlockSpec(memory_space=pltpu.VMEM)
    return pl.pallas_call(
        route_back_kernel,
        in_specs=[pl.BlockSpec(memory_space=pltpu.SMEM)] + [vmem] * 5,
        out_specs=[vmem] * 4,
        out_shape=[
            jax.ShapeDtypeStruct((images, slots, width), jnp.bfloat16),
            jax.ShapeDtypeStruct((images, slots, tokens.shape[1]), jnp.bfloat16),
            jax.ShapeDtypeStruct((slots // 2, width), jnp.bfloat16),
            jax.ShapeDtypeStruct((slots // 2, width), jnp.bfloat16),
        ],
        scratch_shapes=[
            pltpu.VMEM((2 * slots, width), jnp.float32),
            pltpu.VMEM((slots, width), jnp.float32),
        ],
        compiler_params=pltpu.CompilerParams(vmem_limit_bytes=16 << 20),
        name="route_back",
    )(side, back, dispatch, combine, tokens, grad_out)


def token_grad_kernel(disp_ref, slot_ref, dl_ref, par_ref, grad_ref):
    left = jnp.concatenate((disp_ref[0].astype(jnp.bfloat16), dl_ref[0]), axis=0)
    right = jnp.concatenate((slot_ref[0], par_ref[...]), axis=0)
    grad_ref[0] = dot(left, right, TN).astype(jnp.bfloat16)


def token_grads(dispatch, grad_slot, dl, param_t):
    images, slots, patches = dispatch.shape
    width = param_t.shape[1]
    table = pl.BlockSpec((1, slots, patches), lambda i: (i, 0, 0))
    return pl.pallas_call(
        token_grad_kernel,
        grid=(images,),
        in_specs=[
            table,
            pl.BlockSpec((1, slots, width), lambda i: (i, 0, 0)),
            table,
            pl.BlockSpec((slots, width), lambda i: (0, 0)),
        ],
        out_specs=pl.BlockSpec((1, patches, width), lambda i: (i, 0, 0)),
        out_shape=jax.ShapeDtypeStruct((images, patches, width), jnp.bfloat16),
        compiler_params=pltpu.CompilerParams(vmem_limit_bytes=16 << 20),
        name="token_grads",
    )(dispatch, grad_slot, dl, param_t)


def expert_body(
    experts, chunks, place_ref, own_ref, other_ref, first_in, first_out, win_hbm, wout_hbm,
    keep_ref, give_ref, hid_ref, dpre_ref, win_v, wout_v, win_t, wout_t, sems,
):
    place = place_ref[0]
    step = win_v.shape[2] // chunks
    order = [(e, c) for e in range(experts) for c in range(chunks)]
    held = first_in.shape[1] // step

    def copies(k):
        e, c = order[k]
        cols = pl.ds(c * step, step)
        return (
            pltpu.make_async_copy(win_hbm.at[e, :, cols], win_v.at[e, :, cols], sems.at[0, e, c]),
            pltpu.make_async_copy(wout_hbm.at[e, cols, :], wout_v.at[e, cols, :], sems.at[1, e, c]),
        )

    def start(k):
        if k < len(order):
            for copy in copies(k):
                copy.start()

    def weights(k):
        e, c = order[k]
        cols = pl.ds(c * step, step)
        if k < held:
            return first_in.at[:, cols], first_out.at[cols, :]
        return win_v.at[e, :, cols], wout_v.at[e, cols, :]

    groups = {held: 1}
    k = held + 1
    while k < len(order):
        groups[k] = min(2, len(order) - k)
        k += groups[k]

    for k in range(held, held + FLIGHT):
        start(k)
    ready = out = grad = None
    for k in range(len(order) + 1):
        for arriving in range(k, k + groups.get(k, 0)):
            if arriving < len(order):
                for copy in copies(arriving):
                    copy.wait()
                start(arriving + FLIGHT)
        before = ready
        if k < len(order):
            w1, w2 = weights(k)
            e = order[k][0]
            win_t[k] = w1[...].T
            wout_t[k] = w2[...].T
            x, g = by_kind(place, own_ref[e], other_ref[e])
            ready = dot(x, w1[...], NN), dot(g, wout_t[k], NN)
        if before is None:
            continue
        e, c = order[k - 1]
        w2 = weights(k - 1)[1]
        cols = pl.ds(c * step, step)
        pre, back = before
        value, slope = gelu_parts(pre)
        hidden = value.astype(jnp.bfloat16)
        dpre = (back * slope).astype(jnp.bfloat16)
        hid_ref[e, :, cols] = hidden
        dpre_ref[e, :, cols] = dpre
        o = dot(hidden, w2[...], NN)
        d = dot(dpre, win_t[k - 1], NN)
        out, grad = (o, d) if c == 0 else (out + o, grad + d)
        if c == chunks - 1:
            if keep_ref.shape[0] == experts:
                first = place == 0
                keep_ref[e] = jnp.where(first, grad, out)
                give_ref[e] = jnp.where(first, out, grad).astype(jnp.bfloat16)
            else:
                keep_ref[e] = grad
                keep_ref[experts + e] = out
                give_ref[e] = grad.astype(jnp.bfloat16)


def expert_forward(place, own, other, first_in, first_out, weight_in, weight_out, split):
    experts, width, hid = weight_in.shape
    rows = own.shape[1]
    chunks = chunk_count(hid, CHUNKS)
    vmem = pl.BlockSpec(memory_space=pltpu.VMEM)
    hbm = pl.BlockSpec(memory_space=pl.ANY)
    return pl.pallas_call(
        lambda *refs: expert_body(experts, chunks, *refs),
        in_specs=[pl.BlockSpec(memory_space=pltpu.SMEM), vmem, vmem, vmem, vmem, hbm, hbm],
        out_specs=[vmem, vmem, vmem, vmem],
        out_shape=[
            jax.ShapeDtypeStruct((experts if split else 2 * experts, rows, width), jnp.float32),
            jax.ShapeDtypeStruct((experts, rows, width), jnp.bfloat16),
            jax.ShapeDtypeStruct((experts, rows, hid), jnp.bfloat16),
            jax.ShapeDtypeStruct((experts, rows, hid), jnp.bfloat16),
        ],
        scratch_shapes=[
            pltpu.VMEM((experts, width, hid), jnp.bfloat16),
            pltpu.VMEM((experts, hid, width), jnp.bfloat16),
            pltpu.VMEM((experts * chunks, hid // chunks, width), jnp.bfloat16),
            pltpu.VMEM((experts * chunks, width, hid // chunks), jnp.bfloat16),
            pltpu.SemaphoreType.DMA((2, experts, chunks)),
        ],
        compiler_params=pltpu.CompilerParams(vmem_limit_bytes=40 << 20),
        name="expert_forward",
    )(place, own, other, first_in, first_out, in_hbm(weight_in), in_hbm(weight_out))


def weight_grad_kernel(place_ref, own_ref, other_ref, hid_ref, dpre_ref, gin_ref, gout_ref):
    x, g = by_kind(place_ref[0], own_ref[0], other_ref[0])
    gin_ref[0] = dot(x, dpre_ref[0], TN).astype(jnp.bfloat16)
    gout_ref[0] = dot(hid_ref[0], g, TN).astype(jnp.bfloat16)


def weight_grads(place, own, other, hidden, dpre):
    experts, rows, hid = hidden.shape
    width = own.shape[2]
    chunks = chunk_count(hid, 4)
    step = hid // chunks
    return pl.pallas_call(
        weight_grad_kernel,
        grid=(experts, chunks),
        in_specs=[
            pl.BlockSpec(memory_space=pltpu.SMEM),
            pl.BlockSpec((1, rows, width), lambda e, c: (e, 0, 0)),
            pl.BlockSpec((1, rows, width), lambda e, c: (e, 0, 0)),
            pl.BlockSpec((1, rows, step), lambda e, c: (e, 0, c)),
            pl.BlockSpec((1, rows, step), lambda e, c: (e, 0, c)),
        ],
        out_specs=[
            pl.BlockSpec((1, width, step), lambda e, c: (e, 0, c)),
            pl.BlockSpec((1, step, width), lambda e, c: (e, c, 0)),
        ],
        out_shape=[
            jax.ShapeDtypeStruct((experts, width, hid), jnp.bfloat16),
            jax.ShapeDtypeStruct((experts, hid, width), jnp.bfloat16),
        ],
        compiler_params=pltpu.CompilerParams(vmem_limit_bytes=24 << 20),
        name="weight_grads",
    )(place, own, other, hidden, dpre)


def swap(value, axis, mask):
    size = lax.axis_size(axis)
    return lax.ppermute(value, axis, [(k, k ^ mask) for k in range(size)])


def is_pow2(n):
    return n & (n - 1) == 0


def sum_bits(acc, axis, first_bit):
    size = lax.axis_size(axis)
    bit = first_bit
    while bit < size:
        sent = acc.astype(jnp.bfloat16)
        own = sent.astype(jnp.float32)
        if 2 * bit < size:
            got = []
            for mask in (bit, 2 * bit, 3 * bit):
                got.append(swap(sent, axis, mask).astype(jnp.float32))
            a, b, c = got
            acc = (own + a) + (b + c)
            bit *= 4
        else:
            acc = own + swap(sent, axis, bit).astype(jnp.float32)
            bit *= 2
    return acc


def sum_everywhere(keep, give, side):
    ex, ey = lax.axis_size("ex"), lax.axis_size("ey")
    if not (is_pow2(ex) and is_pow2(ey)):
        low = jnp.where(side == 0, keep, give).astype(jnp.float32)
        high = jnp.where(side == 0, give, keep).astype(jnp.float32)
        return lax.psum(jnp.concatenate((low, high), axis=0), ("ex", "ey"))
    acc = keep.astype(jnp.float32) + swap(give, "ex", 1).astype(jnp.float32)
    acc = sum_bits(acc, "ex", 2)
    acc = sum_bits(acc, "ey", 1)
    sent = acc.astype(jnp.bfloat16)
    own = sent.astype(jnp.float32)
    other = swap(sent, "ex", 1)
    other = other.astype(jnp.float32)
    return jnp.concatenate((jnp.where(side == 0, own, other), jnp.where(side == 0, other, own)), axis=0)


def join_kernel(keep_ref, got_ref, sum_hbm, sum_v, sem):
    block, rows, width = keep_ref.shape
    total = (keep_ref[...] + got_ref[...].astype(jnp.float32)).reshape(block * rows, width)
    shape = (block * rows, block * rows)
    to = lax.broadcasted_iota(jnp.int32, shape, 0)
    at = lax.broadcasted_iota(jnp.int32, shape, 1)
    move = jnp.where((to % block) * rows + to // block == at, 1.0, 0.0).astype(jnp.bfloat16)
    moved = dot(move, total.astype(jnp.bfloat16), NN)
    for k in range(rows):
        sum_v[k] = moved[block * k : block * (k + 1)].astype(jnp.bfloat16)
    copy = pltpu.make_async_copy(sum_v, sum_hbm, sem)
    copy.start()
    copy.wait()


def join(keep, got):
    block, rows, width = keep.shape
    vmem = pl.BlockSpec(memory_space=pltpu.VMEM)
    return pl.pallas_call(
        join_kernel,
        in_specs=[vmem, vmem],
        out_specs=pl.BlockSpec(memory_space=pl.ANY),
        out_shape=pltpu.HBM((rows, block, width), jnp.bfloat16),
        scratch_shapes=[pltpu.VMEM((rows, block, width), jnp.bfloat16), pltpu.SemaphoreType.DMA],
        compiler_params=pltpu.CompilerParams(vmem_limit_bytes=16 << 20),
        name="join",
    )(keep, got)


def per_device(tokens, slot_param, weight_in, weight_out, grad_out):
    ex, ey = lax.axis_size("ex"), lax.axis_size("ey")
    images, _, width = tokens.shape
    slots = slot_param.shape[1]
    mine = slots // ey
    param_t = slot_param.T
    sent, dispatch, combine = route_forward(tokens, grad_out, param_t, ey)
    first_in, first_out = fetch_first(weight_in, weight_out)
    side = lax.axis_index("ex") % 2
    rows = ex * ey * images
    paired = ex == 2
    if paired:
        sent = sent.reshape(2 * ey, images * mine, width)
        own = lax.all_to_all(sent, ("ex", "ey"), split_axis=0, concat_axis=0, tiled=True)
        own = own.reshape(rows, mine, width).transpose(1, 0, 2)
        other = swap(own, "ex", 1)
        place = side.reshape(1)
    else:
        place = jnp.zeros((1,), jnp.int32)
        sent = sent.reshape(2, ey, images, mine, width).transpose(1, 2, 0, 3, 4)
        sent = sent.reshape(ey * images, 2 * mine, width)
        moved = lax.all_to_all(sent, "ey", split_axis=0, concat_axis=0, tiled=True)
        arrived = lax.all_gather(moved, "ex", axis=0)
        rows_in = arrived.reshape(rows, 2 * mine, width).transpose(1, 0, 2)
        own, other = rows_in[:mine], rows_in[mine:]
    keep_rows, give_rows, hidden, dpre = expert_forward(
        place, own, other, first_in, first_out, weight_in, weight_out, paired
    )
    if paired:
        summed = join(keep_rows, swap(give_rows, "ex", 1)).reshape(2 * ey, images * mine, width)
        back = lax.all_to_all(summed, ("ex", "ey"), split_axis=0, concat_axis=0, tiled=True)
        back = back.reshape(2 * ey, images, mine, width)
    else:
        blocks = keep_rows.astype(jnp.bfloat16).transpose(1, 0, 2).reshape(ex, ey * images, 2 * mine, width)
        summed = lax.psum_scatter(blocks, "ex", scatter_dimension=0)
        back = lax.all_to_all(summed, "ey", split_axis=0, concat_axis=0, tiled=True)
        back = back.reshape(ey, images, 2, mine, width).transpose(2, 0, 1, 3, 4)
        back = back.reshape(2 * ey, images, mine, width)
    grad_win, grad_wout = weight_grads(place, own, other, hidden, dpre)
    grad_slot, logit_grad, keep, give = route_back(side.reshape(1), back, dispatch, combine, tokens, grad_out)
    grad_param = sum_everywhere(keep, give, side).T
    grad_tokens = token_grads(dispatch, grad_slot, logit_grad, param_t)
    return (grad_tokens, grad_param, grad_win, grad_wout)


def solution(mesh):
    in_specs = (
        P(("ex", "ey"), None, None),
        P(),
        P("ey", None, "ex"),
        P("ey", "ex", None),
        P(("ex", "ey"), None, None),
    )
    out_specs = (P(("ex", "ey"), None, None), P(), P("ey", None, "ex"), P("ey", "ex", None))

    return jax.shard_map(per_device, mesh=mesh, in_specs=in_specs, out_specs=out_specs, check_vma=False)
```
